32 devices in a mesh: blk: 2 (over x), wide: 16 (over z, y, core).
Axes of the slice: x: 2, y: 2, z: 4, core: 2. Of those that a mesh axis runs over, the one named last changes fastest.
Arguments:
- resid: bfloat16 [8192, 1024], P('wide', 'blk'), may hold values from -24 to 24
- samples: bfloat16 [8192, 1024], P('wide', 'blk'), may hold values from -6 to 6
- precision: float32 [64, 2, 32, 128, 128], P('wide', 'blk'), as said below
- active: int32 [64, 2, 32], P('wide', 'blk'), may hold values 0 or 1
Outputs:
- updated: float32 [64, 2, 32, 128, 128], P('wide', 'blk')
The draws below stay inside these ranges and needn't reach their ends.
Inputs may be any that keep to these rules, and one draw needn't show every extreme that they name: `precision`: entries on the diagonal of W lie between 1 and 2.
All inputs are finite; a program needn't handle non-finite values. No bound on the sum of `active` on one device may be relied on, other than what follows from the above.
Results may differ from the reference program's by a relative error of at most 0.0003.
Values may be sent and summed in bfloat16 or wider, within the bound.
A program may use at most 192 MiB of HBM per device.

```python
import jax
import jax.numpy as jnp
from jax import lax

P_SIZE = 8192
TILE = 128
N = 1024
TILES = 64
TPC = 32
N_BLK = 2


def draw_precision(key, part):
    first_key, second_key = jax.random.split(key, 2)
    full_shape = (TILES, N_BLK, TPC, TILE, TILE)
    off_part = 0.1 * jax.random.normal(first_key, full_shape, jnp.float32)
    diag_part = jax.random.uniform(second_key, full_shape, jnp.float32, 1.0, 2.0)
    row_tile = lax.broadcasted_iota(jnp.int32, full_shape, 0)
    class_index = lax.broadcasted_iota(jnp.int32, full_shape, 1)
    within_index = lax.broadcasted_iota(jnp.int32, full_shape, 2)
    inner_row = lax.broadcasted_iota(jnp.int32, full_shape, 3)
    inner_column = lax.broadcasted_iota(jnp.int32, full_shape, 4)
    column_tile = (class_index - row_tile) % N_BLK + N_BLK * within_index
    on_diag = (column_tile == row_tile) & (inner_row == inner_column)
    return jnp.where(on_diag, diag_part, off_part)


def place_ends(drawn, rng, low, top_value):
    place = [jax.random.randint(jax.random.fold_in(rng, axis), (), 0, length) for axis, length in enumerate(drawn.shape)]
    main_axis = drawn.shape.index(max(drawn.shape))
    neighbour = place[:main_axis] + [(place[main_axis] + 1) % drawn.shape[main_axis]] + place[main_axis + 1:]
    return drawn.at[tuple(place)].set(low).at[tuple(neighbour)].set(top_value)


def block_levels(stream_key, dims, shards, smallest, top_value):
    def one(dim, parts):
        steps = jax.random.uniform(jax.random.fold_in(jax.random.fold_in(stream_key, 6), dim), (parts,), jnp.float32, smallest / len(shards), top_value / len(shards))
        return jnp.repeat(jnp.exp(steps), dims[dim] // parts).reshape((-1,) + (1,) * (len(dims) - dim - 1))

    gain = one(*shards[0])
    for cut in shards[1:]:
        gain = gain * one(*cut)
    return gain


def scatter_about(own_key, dims, deviation, most, shards=(), kind=jnp.bfloat16):
    result = deviation * jax.random.normal(own_key, dims, jnp.float32)
    if shards:
        result = result * block_levels(own_key, dims, shards, -0.22, 0.18)
    return jnp.clip(result, -most, most).astype(kind)


def setup_inputs(seed: int = 0) -> dict:
    seeds = jax.random.split(jax.random.key(seed), 5)
    return {
        "resid": scatter_about(seeds[0], (P_SIZE, N), 4.0, 24.0, ((0, 16), (1, 2))),
        "samples": scatter_about(seeds[1], (P_SIZE, N), 1.0, 6.0, ((0, 16), (1, 2))),
        "precision": draw_precision(jax.random.fold_in(seeds[4], 71), 0),
        "active": place_ends((jax.random.randint(seeds[3], (TILES, N_BLK, TPC), 0, 4) < 3).astype(jnp.int32), jax.random.fold_in(seeds[3], 1), 0, 1),
    }


STEP = 1.0
LASSO = 0.1
RIDGE = 0.5


def class_columns(row_ids, groups, per_class):
    classes = jnp.arange(groups, dtype=jnp.int32)
    within = jnp.arange(per_class, dtype=jnp.int32)
    return (classes[None, :, None] - row_ids[:, None, None]) % groups + groups * within[None, None, :]


def reference(resid, samples, precision, active):
    total_samples = resid.shape[1]
    tiles = precision.shape[0]
    groups = precision.shape[1]
    per_class = precision.shape[2]
    tile_size = precision.shape[3]
    gram = jnp.dot(resid, samples.T, preferred_element_type=jnp.float32) / total_samples
    gram_tiles = gram.reshape(tiles, tile_size, tiles, tile_size).transpose(0, 2, 1, 3)
    row_ids = jnp.arange(tiles, dtype=jnp.int32)
    column_ids = class_columns(row_ids, groups, per_class)
    forward = gram_tiles[row_ids[:, None, None], column_ids]
    backward = jnp.swapaxes(gram_tiles[column_ids, row_ids[:, None, None]], 3, 4)
    symmetric = 0.5 * (forward + backward)
    same_tile = column_ids == row_ids[:, None, None]
    identity = jnp.eye(tile_size, dtype=bool)
    on_diag = same_tile[:, :, :, None, None] & identity
    inverse = jnp.where(on_diag, 1.0 / jnp.where(on_diag, precision, 1.0), 0.0)
    stepped = precision - STEP * (symmetric + RIDGE * precision - inverse)
    shrunk = jnp.sign(stepped) * jnp.maximum(jnp.abs(stepped) - STEP * LASSO, 0.0)
    active_flags = active.astype(precision.dtype)
    return jnp.where(on_diag, stepped, shrunk) * active_flags[:, :, :, None, None]
```

```python
import functools

import jax
import jax.numpy as jnp
from jax import lax
from jax.experimental import pallas as pl
from jax.experimental.pallas import tpu as pltpu
from jax.sharding import PartitionSpec as P

STEP = 1.0
LASSO = 0.1
RIDGE = 0.5


def local(resid, samples, precision, active):
    groups = lax.axis_size("blk")
    column_group = lax.axis_index("blk")
    panel_index = lax.axis_index("wide")
    row_tiles = precision.shape[0]
    per_class = precision.shape[2]
    tile_size = precision.shape[3]
    tiles = per_class * groups
    local_samples = resid.shape[1]
    total_samples = local_samples * groups
    own_rows = panel_index * row_tiles + jnp.arange(row_tiles, dtype=jnp.int32)
    first_column = (column_group - own_rows) % groups
    own_resid = resid.reshape(row_tiles, tile_size, local_samples)
    own_data = samples.reshape(row_tiles, tile_size, local_samples)
    all_resid, all_data = (
        lax.all_gather(resid, "wide", axis=0, tiled=True),
        lax.all_gather(samples, "wide", axis=0, tiled=True),
    )
    resid_tiles = all_resid.reshape(tiles, tile_size, local_samples)
    data_tiles = all_data.reshape(tiles, tile_size, local_samples)
    positions = jnp.arange(per_class * lax.axis_size("blk"), dtype=jnp.int32)
    classes = positions // per_class
    within = positions % per_class
    column_ids = (classes[:, None] - own_rows[None, :]) % groups + groups * within[:, None]
    forward = jnp.einsum(
        "kis,pkjs->pkij", own_resid, data_tiles[column_ids], preferred_element_type=jnp.float32
    )
    backward = jnp.einsum(
        "kis,pkjs->pkij", own_data, resid_tiles[column_ids], preferred_element_type=jnp.float32
    )
    summed = (
        lax.psum_scatter(0.5 * (forward + backward), "blk", scatter_dimension=0, tiled=True)
        / total_samples
    )
    precision_tiles = precision[:, 0]
    active_flags = active[:, 0].astype(jnp.float32)
    gradient_part = summed.transpose(1, 0, 2, 3)
    column_ids = first_column[:, None] + groups * jnp.arange(per_class, dtype=jnp.int32)[None, :]
    same_tile = column_ids == own_rows[:, None]
    identity = jnp.eye(tile_size, dtype=bool)
    on_diag = same_tile[:, :, None, None] & identity
    inverse = jnp.where(on_diag, 1.0 / jnp.where(on_diag, precision_tiles, 1.0), 0.0)
    stepped = precision_tiles - STEP * (gradient_part + RIDGE * precision_tiles - inverse)
    shrunk = jnp.sign(stepped) * jnp.maximum(jnp.abs(stepped) - STEP * LASSO, 0.0)
    updated = jnp.where(on_diag, stepped, shrunk) * active_flags[:, :, None, None]
    return updated[:, None]


MESH = pl.DeviceIdType.MESH

END = (
    (1, 0, 0, 0, 1, 1), (0, 1, 0, 1, 0, 1), (1, 0, 1, 0, 1, 0), (0, 1, 1, 1, 0, 0),
    (2, 0, 0, 0, 1, 1), (1, 1, 0, 0, 0, 1), (2, 0, 1, 0, 1, 1), (1, 1, 1, 0, 0, 1),
    (3, 0, 0, 0, 0, 1), (2, 1, 0, 0, 0, 1), (3, 0, 1, 0, 1, 1), (2, 1, 1, 0, 0, 1),
    (3, 1, 0, 0, 0, 1), (3, 1, 1, 0, 0, 1),
)
INNER = (
    (2, 0, 0, 2, 1, 1), (0, 0, 0, 1, 0, 1), (1, 1, 0, 0, 0, 1), (2, 0, 1, 2, 1, 1),
    (0, 0, 1, 1, 0, 0), (1, 1, 1, 0, 0, 0), (3, 0, 0, 2, 0, 1), (0, 1, 0, 1, 0, 1),
    (2, 1, 0, 0, 0, 1), (3, 0, 1, 2, 0, 1), (0, 1, 1, 1, 0, 1), (2, 1, 1, 0, 0, 1),
    (3, 1, 0, 2, 0, 1), (3, 1, 1, 0, 0, 1),
)
STEPS = len(END)
EARLY = 4
LAG = 6
OWN = STEPS


def packed(row):
    place, across, u, along, over, handed = row
    return place + 4 * across + 8 * u + 16 * along + 64 * over + 128 * handed


def kernel(
    depth, scale, resid, samples, weights, flags, held,
    own, cols, beside, near, stage, landed, recv, own_recv, res_recv, beside_recv, near_recv, send,
    own_send, res_send, beside_send, near_send, fill,
):
    b = lax.axis_index("blk")
    w = lax.axis_index("wide")
    nb = 1 - b
    z, y, c = w // 4, (w // 2) % 2, w % 2
    per = own.shape[2]
    tile = own.shape[4]
    last = depth - 1
    half = z // 2
    inner = jnp.where(z == 0, 0, jnp.where(z == last, 0, 1))
    inward = z + 1 - 2 * half
    outward = jnp.where(inner == 1, z - 1 + 2 * half, inward)

    def at(zz, yy, cc):
        return (zz * 2 + yy) * 2 + cc

    in_target, out_target = at(inward, y, c), at(outward, y, c)
    y_target, c_target = at(z, 1 - y, c), at(z, y, 1 - c)
    pair_target = jnp.where(inner == 1, out_target, in_target)

    def decode(n):
        end, mid = jnp.int32(packed(END[0])), jnp.int32(packed(INNER[0]))
        for k in range(1, STEPS):
            end = jnp.where(n == k, jnp.int32(packed(END[k])), end)
            mid = jnp.where(n == k, jnp.int32(packed(INNER[k])), mid)
        code = jnp.where(inner == 1, mid, end)
        place = code % 4
        zz = jnp.where(half == 0, place, last - place)
        yy = jnp.where((code // 4) % 2 == 1, 1 - y, y)
        u = (code // 8) % 2
        along = (code // 16) % 4
        over = (code // 64) % 2
        handed = code // 128
        return at(zz, yy, c), at(zz, yy, 1 - c), u, along, over, handed

    loads = []
    for a, src in enumerate((resid, samples)):
        for p in range(2):
            loads.append(
                pltpu.make_async_copy(src.at[:, p], own.at[b, p, :, a], fill.at[2 * a + p])
            )
    for load in loads:
        load.start()
    load_weights = pltpu.make_async_copy(weights, held, fill.at[4])

    barrier = pltpu.get_barrier_semaphore()

    def greet(**device):
        pl.semaphore_signal(barrier, inc=1, device_id=device, device_id_type=MESH)

    greet(blk=nb)
    greet(wide=y_target)
    greet(wide=c_target)
    greet(wide=in_target)

    @pl.when(inner == 1)
    def _():
        greet(wide=out_target)

    pl.semaphore_wait(barrier, 4 + inner)

    def push(h, u, src, panel, k, lane, target):
        return pltpu.make_async_remote_copy(
            src_ref=src, dst_ref=cols.at[h, panel, u], send_sem=send.at[h, u, k, lane],
            recv_sem=recv.at[h, panel, u], device_id={"wide": target}, device_id_type=MESH,
        )

    def arrive(h, u, panel):
        push(h, u, cols.at[h, panel, u], panel, 0, 0, y_target).wait_recv()

    def own_pushes(h, u):
        src = own.at[h, b, u]
        return (
            (None, push(h, u, src, w, OWN, 2, y_target)),
            (None, push(h, u, src, w, OWN, 0, in_target)),
            (inner == 1, push(h, u, src, w, OWN, 1, out_target)),
            (None, push(h, u, src, w, OWN, 3, c_target)),
        )

    def step_pushes(h, n, step):
        panel, _, u, along, over, _ = step
        src = cols.at[h, panel, u]
        target = jnp.where(along == 1, in_target, out_target)
        return (
            (along > 0, push(h, u, src, panel, n, 0, target)),
            (over == 1, push(h, u, src, panel, n, 2, y_target)),
            (None, push(h, u, src, panel, n, 3, c_target)),
        )

    def beside_push(h):
        return ((None, pltpu.make_async_remote_copy(
            src_ref=own.at[h, nb], dst_ref=beside.at[h], send_sem=beside_send.at[h],
            recv_sem=beside_recv.at[h], device_id={"wide": c_target}, device_id_type=MESH,
        )),)

    def near_push(h, j, src, target):
        return ((None, pltpu.make_async_remote_copy(
            src_ref=src, dst_ref=near.at[h, j], send_sem=near_send.at[h, j],
            recv_sem=near_recv.at[h, j], device_id={"wide": target}, device_id_type=MESH,
        )),)

    def near_own(h, j):
        return near_push(h, j, own.at[h, nb, per - 1], y_target if j == 0 else pair_target)

    def near_relay(h, j):
        return near_push(h, j + 1, near.at[h, j], c_target)

    def near_arrive(h, j):
        near_push(h, j, near.at[h, j], c_target)[0][1].wait_recv()

    def start(pushes):
        for when, copy in pushes:
            if when is None:
                copy.start()
            else:
                pl.when(when)(copy.start)

    def drain(pushes):
        for when, copy in pushes:
            if when is None:
                copy.wait_send()
            else:
                pl.when(when)(copy.wait_send)

    def swap(h, i, t):
        p = (nb, b)[i] if h is b else (b, nb)[i]
        return pltpu.make_async_remote_copy(
            src_ref=own.at[h, p, t], dst_ref=own.at[h, p, t], send_sem=own_send.at[i, t],
            recv_sem=own_recv.at[i, t], device_id={"blk": nb}, device_id_type=MESH,
        )

    def hand(panel, u):
        return pltpu.make_async_remote_copy(
            src_ref=stage.at[panel, u], dst_ref=landed.at[panel, u],
            send_sem=res_send.at[panel, u], recv_sem=res_recv.at[panel, u],
            device_id={"blk": nb}, device_id_type=MESH,
        )

    def gram(p, side):
        total = None
        for h in range(2):
            for a in range(2):
                left = own[h, p, :, a].reshape(per * tile, -1)
                right = side(h, 1 - a).reshape(-1, own.shape[5])
                part = lax.dot_general(
                    left, right, (((1,), (1,)), ((), ())), preferred_element_type=jnp.float32
                )
                total = part if total is None else total + part
        return total * scale

    def finish(p, panel, u, part, diagonal=False):
        for t in range(per):
            slot = panel * per + u
            weight = held[t, p, slot]
            half = part(t) + RIDGE * weight
            if diagonal and t == u:
                rows = lax.broadcasted_iota(jnp.int32, (tile, tile), 0)
                columns = lax.broadcasted_iota(jnp.int32, (tile, tile), 1)
                on_diag = rows == columns + b * (2 * tile)
                inverse = jnp.where(on_diag, 1.0 / jnp.where(on_diag, weight, 1.0), 0.0)
                stepped = weight - STEP * (half - inverse)
            else:
                stepped = weight - STEP * half
            bound = STEP * LASSO
            updated = stepped - jnp.clip(stepped, -bound, bound)
            if diagonal and t == u:
                updated = jnp.where(on_diag, stepped, updated)
            flag = flags[2 * t + p, slot].astype(jnp.float32)
            held[t, p, slot] = updated * flag

    def cut(total, u=0):
        return lambda t: total[t * tile:(t + 1) * tile, u * tile:(u + 1) * tile]

    def finish_all(p, panel, total, diagonal=False):
        for u in range(per):
            finish(p, panel, u, cut(total, u), diagonal)

    def keep(panel):
        finish_all(0, panel, gram(0, lambda h, a: cols[h, panel, :, a]))

    def forward(n):
        step = decode(n)
        for h in (b, nb):
            arrive(h, step[2], step[0])
            start(step_pushes(h, n, step))

    for load in loads:
        load.wait()
    for i in range(2):
        for t in range(per):
            swap(b, i, t).start()
    for t in range(per):
        start(own_pushes(b, t))
    load_weights.start()
    start(beside_push(b))
    for t in range(per):
        swap(nb, 0, t).wait_recv()
        start(own_pushes(nb, t))

    def early(n, carry):
        forward(n)
        return carry

    lax.fori_loop(0, EARLY, early, 0)
    for t in range(per):
        swap(nb, 1, t).wait_recv()
    start(beside_push(nb))
    load_weights.wait()

    def receive(n):
        first, second, u, _, _, handed = decode(n)

        @pl.when(handed == 1)
        def _():
            for panel in (first, second):
                hand(panel, u).wait_recv()
                finish(1, panel, u, lambda t: landed[panel, u, t])

    def nearby():
        for p in range(2):
            parity = b if p == 0 else nb
            finish_all(p, w, gram(p, lambda h, a: own[h, parity, :, a]), True)
        for h in (b, nb):
            for u in range(per):
                arrive(h, u, c_target)
            beside_push(h)[0][1].wait_recv()
        keep(c_target)
        finish_all(1, c_target, gram(1, lambda h, a: beside[h, :, a]))

    def compute(n, carry):
        @pl.when(n >= EARLY)
        def _():
            forward(n)

        first, second, u, _, _, handed = decode(n)

        @pl.when(n == jnp.where(inner == 1, STEPS - 2, STEPS - 4))
        def _():
            for h in (b, nb):
                start(near_own(h, 0))
                start(near_own(h, 2))

        def both(i, carry):
            panel = jnp.where(i == 0, first, second)

            @pl.when(i == 1)
            def _():
                for h in (b, nb):
                    arrive(h, u, panel)

            @pl.when(handed == 1)
            def _():
                total = cut(gram(1, lambda h, a: cols[h, panel, u, a]))
                for t in range(per):
                    stage[panel, u, t] = total(t)
                hand(panel, u).start()

            @pl.when(u == per - 1)
            def _():
                keep(panel)

            return carry

        lax.fori_loop(0, 2, both, 0)

        @pl.when(n == EARLY - 1)
        def _():
            nearby()

        @pl.when(n >= LAG)
        def _():
            receive(n - LAG)

        return carry

    lax.fori_loop(0, STEPS, compute, 0)

    def settle(n, carry):
        receive(n)
        return carry

    lax.fori_loop(STEPS - LAG, STEPS - 2, settle, 0)

    for h in (b, nb):
        for j in (0, 2):
            near_arrive(h, j)
            start(near_relay(h, j))

    beyond = jnp.where(inner == 1, outward, inward)

    def adjacent(i, carry):
        j = jnp.where(i < 2, 2 * i, 2 * i - 3)
        zz = jnp.where(j < 2, z, beyond)
        yy = jnp.where(j < 2, 1 - y, y)
        cc = jnp.where(j % 2 == 0, c, 1 - c)

        @pl.when(i >= 2)
        def _():
            for h in (b, nb):
                near_arrive(h, j)

        total = gram(1, lambda h, a: near[h, j, a])
        finish(1, at(zz, yy, cc), per - 1, cut(total))
        return carry

    lax.fori_loop(0, 4, adjacent, 0)
    lax.fori_loop(STEPS - 2, STEPS, settle, 0)

    for i in range(2):
        for t in range(per):
            swap(b, i, t).wait_send()
    for h in (b, nb):
        for t in range(per):
            drain(own_pushes(h, t))
        drain(beside_push(h))
        for j in (0, 2):
            drain(near_own(h, j))
            drain(near_relay(h, j))

    def drain_step(n, carry):
        step = decode(n)
        for h in (b, nb):
            drain(step_pushes(h, n, step))

        @pl.when(step[5] == 1)
        def _():
            for panel in step[:2]:
                hand(panel, step[2]).wait_send()

        return carry

    lax.fori_loop(0, STEPS, drain_step, 0)


def ring(resid, samples, precision, active):
    panels = lax.axis_size("wide")
    row_tiles, _, per_class, tile, _ = precision.shape
    per = row_tiles // 2
    half = resid.shape[1]
    depth = panels // 4
    scale = 0.5 / (2 * half)
    any_spec = pl.BlockSpec(memory_space=pl.ANY)
    bf16, f32 = resid.dtype, jnp.float32
    dma = pltpu.SemaphoreType.DMA
    updated = pl.pallas_call(
        functools.partial(kernel, depth, scale),
        out_shape=pltpu.VMEM((per, 2, per_class, tile, tile), f32),
        in_specs=[any_spec, any_spec, any_spec, pl.BlockSpec(memory_space=pltpu.SMEM)],
        out_specs=pl.BlockSpec(memory_space=pltpu.VMEM),
        scratch_shapes=[
            pltpu.VMEM((2, 2, per, 2, tile, half), bf16),
            pltpu.VMEM((2, panels, per, 2, tile, half), bf16),
            pltpu.VMEM((2, per, 2, tile, half), bf16),
            pltpu.VMEM((2, 4, 2, tile, half), bf16),
            pltpu.VMEM((panels, per, per, tile, tile), f32),
            pltpu.VMEM((panels, per, per, tile, tile), f32),
            dma((2, panels, per)),
            dma((2, per)),
            dma((panels, per)),
            dma((2,)),
            dma((2, 4)),
            dma((2, per, STEPS + 1, 4)),
            dma((2, per)),
            dma((panels, per)),
            dma((2,)),
            dma((2, 4)),
            dma((5,)),
        ],
        compiler_params=pltpu.CompilerParams(
            collective_id=0, has_side_effects=True, vmem_limit_bytes=52 * 1024 * 1024
        ),
    )(
        resid.reshape(per, 2, tile, half),
        samples.reshape(per, 2, tile, half),
        precision.reshape(per, 2, per_class, tile, tile),
        active[:, 0],
    )
    return updated.reshape(precision.shape)


def body(resid, samples, precision, active):
    panels = lax.axis_size("wide")
    row_tiles, _, per_class, tile, _ = precision.shape
    words = 8 * per_class * row_tiles * tile * tile + 4 * panels * row_tiles * tile * resid.shape[1]
    if lax.axis_size("blk") == 2 and panels // 4 == 4 and row_tiles == 4 and words < 52 * 1024 * 1024:
        return ring(resid, samples, precision, active)
    return local(resid, samples, precision, active)


def solution(mesh):
    in_specs = (
        P("wide", "blk"),
        P("wide", "blk"),
        P("wide", "blk", None, None, None),
        P("wide", "blk", None),
    )
    out_specs = P("wide", "blk", None, None, None)
    return jax.shard_map(body, mesh=mesh, in_specs=in_specs, out_specs=out_specs, check_vma=False)
```

```python
import functools

import jax
import jax.numpy as jnp
from jax import lax
from jax.experimental import pallas as pl
from jax.experimental.pallas import tpu as pltpu
from jax.sharding import PartitionSpec as P

STEP = 1.0
LASSO = 0.1
RIDGE = 0.5


def local(resid, samples, precision, active):
    groups = lax.axis_size("blk")
    column_group = lax.axis_index("blk")
    panel_index = lax.axis_index("wide")
    row_tiles = precision.shape[0]
    per_class = precision.shape[2]
    tile_size = precision.shape[3]
    tiles = per_class * groups
    local_samples = resid.shape[1]
    total_samples = local_samples * groups
    own_rows = panel_index * row_tiles + jnp.arange(row_tiles, dtype=jnp.int32)
    first_column = (column_group - own_rows) % groups
    own_resid = resid.reshape(row_tiles, tile_size, local_samples)
    own_data = samples.reshape(row_tiles, tile_size, local_samples)
    all_resid, all_data = (
        lax.all_gather(resid, "wide", axis=0, tiled=True),
        lax.all_gather(samples, "wide", axis=0, tiled=True),
    )
    resid_tiles = all_resid.reshape(tiles, tile_size, local_samples)
    data_tiles = all_data.reshape(tiles, tile_size, local_samples)
    positions = jnp.arange(per_class * lax.axis_size("blk"), dtype=jnp.int32)
    classes = positions // per_class
    within = positions % per_class
    column_ids = (classes[:, None] - own_rows[None, :]) % groups + groups * within[:, None]
    forward = jnp.einsum(
        "kis,pkjs->pkij", own_resid, data_tiles[column_ids], preferred_element_type=jnp.float32
    )
    backward = jnp.einsum(
        "kis,pkjs->pkij", own_data, resid_tiles[column_ids], preferred_element_type=jnp.float32
    )
    summed = (
        lax.psum_scatter(0.5 * (forward + backward), "blk", scatter_dimension=0, tiled=True)
        / total_samples
    )
    precision_tiles = precision[:, 0]
    active_flags = active[:, 0].astype(jnp.float32)
    gradient_part = summed.transpose(1, 0, 2, 3)
    column_ids = first_column[:, None] + groups * jnp.arange(per_class, dtype=jnp.int32)[None, :]
    same_tile = column_ids == own_rows[:, None]
    identity = jnp.eye(tile_size, dtype=bool)
    on_diag = same_tile[:, :, None, None] & identity
    inverse = jnp.where(on_diag, 1.0 / jnp.where(on_diag, precision_tiles, 1.0), 0.0)
    stepped = precision_tiles - STEP * (gradient_part + RIDGE * precision_tiles - inverse)
    shrunk = jnp.sign(stepped) * jnp.maximum(jnp.abs(stepped) - STEP * LASSO, 0.0)
    updated = jnp.where(on_diag, stepped, shrunk) * active_flags[:, :, None, None]
    return updated[:, None]


MESH = pl.DeviceIdType.MESH

END = (
    (1, 0, 0, 0, 1, 0, 2), (0, 1, 0, 1, 0, 1, 0), (0, 1, 1, 1, 0, 1, 1), (2, 0, 0, 0, 1, 1, 0),
    (2, 0, 1, 0, 1, 1, 1), (1, 1, 0, 0, 0, 1, 2), (3, 0, 0, 0, 1, 1, 0), (2, 1, 0, 0, 0, 1, 0),
    (3, 0, 1, 0, 1, 1, 1), (2, 1, 1, 0, 0, 1, 1), (3, 1, 0, 0, 0, 1, 0), (3, 1, 1, 0, 0, 1, 1),
)
INNER = (
    (2, 0, 0, 2, 1, 1, 0), (0, 0, 0, 1, 0, 1, 0), (1, 1, 0, 0, 0, 0, 0), (2, 0, 1, 2, 1, 0, 1),
    (0, 0, 1, 1, 0, 1, 1), (1, 1, 1, 0, 0, 0, 1), (3, 0, 0, 2, 0, 1, 0), (0, 1, 0, 1, 0, 1, 0),
    (2, 1, 0, 0, 0, 1, 0), (3, 0, 1, 2, 0, 1, 1), (0, 1, 1, 1, 0, 1, 1), (2, 1, 1, 0, 0, 1, 1),
    (3, 1, 0, 0, 0, 1, 0), (3, 1, 1, 0, 0, 1, 1),
)
STEPS = len(INNER)
EARLY = (3, 6)
LAG = 4
BATCH = 8
ALONG, OVER, CORE, HAND, SWAP, BESIDE, NEAR, PAIR, DIRECT, VIA, ONWARD = range(11)


def packed(row):
    place, across, u, along, over, handed, kept = row
    return place + 4 * across + 8 * u + 16 * along + 64 * over + 128 * handed + 256 * kept


def kernel(
    depth, scale, resid, samples, weights, flags, held,
    own, cols, beside, near, pair, stage, landed, out, got, passing, recv, beside_cols, own_recv,
    res_recv, beside_recv, near_recv, pair_recv, got_recv, passing_recv, sends, fill,
):
    b = lax.axis_index("blk")
    w = lax.axis_index("wide")
    nb = 1 - b
    z, y, c = w // 4, (w // 2) % 2, w % 2
    per = own.shape[2]
    tile = own.shape[4]
    last = depth - 1
    half = z // 2
    inner = jnp.where(z == 0, 0, jnp.where(z == last, 0, 1))
    inward = z + 1 - 2 * half
    outward = jnp.where(inner == 1, z - 1 + 2 * half, inward)

    def at(zz, yy, cc):
        return (zz * 2 + yy) * 2 + cc

    in_target, out_target = at(inward, y, c), at(outward, y, c)
    y_target, c_target = at(z, 1 - y, c), at(z, y, 1 - c)
    count = len(END) + (len(INNER) - len(END)) * inner
    ahead = EARLY[0] + (EARLY[1] - EARLY[0]) * inner

    def decode(n):
        end, mid = jnp.int32(packed(END[0])), jnp.int32(packed(INNER[0]))
        for k in range(1, STEPS):
            if k < len(END):
                end = jnp.where(n == k, jnp.int32(packed(END[k])), end)
            mid = jnp.where(n == k, jnp.int32(packed(INNER[k])), mid)
        code = jnp.where(inner == 1, mid, end)
        place = code % 4
        zz = jnp.where(half == 0, place, last - place)
        across = (code // 4) % 2
        yy = jnp.where(across == 1, 1 - y, y)
        u = (code // 8) % 2
        along = (code // 16) % 4
        over = (code // 64) % 2
        handed = (code // 128) % 2
        kept = code // 256
        served = jnp.where(place == 0, inner, 0)
        return at(zz, yy, c), at(zz, yy, 1 - c), u, along, over, handed, kept, across, served

    loads = []
    for a, src in enumerate((resid, samples)):
        for p in range(2):
            loads.append(
                pltpu.make_async_copy(src.at[:, p], own.at[b, p, :, a], fill.at[0])
            )
    for load in loads:
        load.start()
    load_weights = pltpu.make_async_copy(weights, held, fill.at[1])

    barrier = pltpu.get_barrier_semaphore()

    def greet(**device):
        pl.semaphore_signal(barrier, inc=1, device_id=device, device_id_type=MESH)

    greet(blk=nb)
    greet(wide=y_target)
    greet(wide=c_target)
    greet(wide=in_target)

    @pl.when(inner == 1)
    def _():
        greet(wide=out_target)

    greet(wide=at(outward, y, 1 - c))
    pl.semaphore_wait(barrier, 5 + inner)

    def whole(ref, sent_sem, took_sem):
        return pltpu.make_async_remote_copy(
            src_ref=ref, dst_ref=ref, send_sem=sent_sem, recv_sem=took_sem,
            device_id={"wide": y_target}, device_id_type=MESH,
        )

    def took(ref, sem):
        whole(ref, sends.at[0], sem).wait_recv()

    def sent(ref, k):
        whole(ref, sends.at[k], recv.at[0, 0, 0]).wait_send()

    def push(h, u, src, panel, lane, target):
        sem = beside_cols.at[panel // 2, u] if lane == CORE else recv.at[h, panel // 2, u]
        return pltpu.make_async_remote_copy(
            src_ref=src, dst_ref=cols.at[h, panel, u], send_sem=sends.at[lane],
            recv_sem=sem, device_id={"wide": target}, device_id_type=MESH,
        )

    def arrive(h, u, panel):
        took(cols.at[h, panel, u], recv.at[h, panel // 2, u])

    def arrive_beside(u, panel):
        took(cols.at[:, panel, u], beside_cols.at[panel // 2, u])

    def own_pushes(h, u):
        src = own.at[h, b, u]
        return (
            (None, push(h, u, src, w, OVER, y_target)),
            (None, push(h, u, src, w, ALONG, in_target)),
            (None, push(h, u, src, w, CORE, c_target)),
        ) + (((inner == 1, push(h, u, src, w, ALONG, out_target)),) if u == 0 else ())

    def step_pushes(h, step):
        panel, _, u, along, over = step[:5]
        src = cols.at[h, panel, u]
        target = jnp.where(along == 1, in_target, out_target)
        return (
            (along > 0, push(h, u, src, panel, ALONG, target)),
            (over == 1, push(h, u, src, panel, OVER, y_target)),
            (None, push(h, u, src, panel, CORE, c_target)),
        )

    def beside_push(h):
        return ((None, pltpu.make_async_remote_copy(
            src_ref=own.at[h, nb], dst_ref=beside.at[h], send_sem=sends.at[BESIDE],
            recv_sem=beside_recv.at[0], device_id={"wide": c_target}, device_id_type=MESH,
        )),)

    def near_push(h, d, u, src, target):
        return ((None, pltpu.make_async_remote_copy(
            src_ref=src, dst_ref=near.at[h, d, u], send_sem=sends.at[NEAR],
            recv_sem=near_recv.at[u if d == 0 else 2], device_id={"wide": target}, device_id_type=MESH,
        )),)

    def near_own(h, u):
        return near_push(h, 0, u, own.at[h, nb, u], y_target)

    def near_relay(h, u):
        return near_push(h, 1, u, near.at[h, 0, u], c_target)

    def near_arrive(u):
        took(near.at[:, 0, u], near_recv.at[u])

    def pair_push(h, d, src, target):
        return ((None, pltpu.make_async_remote_copy(
            src_ref=src, dst_ref=pair.at[h, d], send_sem=sends.at[PAIR],
            recv_sem=pair_recv.at[d], device_id={"wide": target}, device_id_type=MESH,
        )),)

    def pair_own(h):
        return pair_push(h, 0, own.at[h, nb, per - 1], in_target)

    def pair_relay(h):
        return pair_push(h, 1, pair.at[h, 0], c_target)

    def pair_arrive(d):
        took(pair.at[:, d], pair_recv.at[d])

    def outward_core(d):
        return at(outward, y, jnp.where(d == 0, c, 1 - c))

    def direct(d, p, u, t):
        return pltpu.make_async_remote_copy(
            src_ref=out.at[0, d, p, u, t], dst_ref=got.at[d, p, u, t],
            send_sem=sends.at[DIRECT], recv_sem=got_recv.at[0],
            device_id={"wide": outward_core(d)}, device_id_type=MESH,
        )

    def via(d, p, u):
        return pltpu.make_async_remote_copy(
            src_ref=out.at[1, d, p, u, per - 1], dst_ref=passing.at[d, p, u],
            send_sem=sends.at[VIA], recv_sem=passing_recv.at[p * (1 + u)],
            device_id={"wide": y_target}, device_id_type=MESH,
        )

    def onward(d, p, u):
        return pltpu.make_async_remote_copy(
            src_ref=passing.at[d, p, u], dst_ref=got.at[2 + d, p, u, per - 1],
            send_sem=sends.at[ONWARD], recv_sem=got_recv.at[1],
            device_id={"wide": outward_core(d)}, device_id_type=MESH,
        )

    def start(pushes):
        for when, copy in pushes:
            if when is None:
                copy.start()
            else:
                pl.when(when)(copy.start)

    def swap(h, i, t):
        p = (nb, b)[i] if h is b else (b, nb)[i]
        return pltpu.make_async_remote_copy(
            src_ref=own.at[h, p, t], dst_ref=own.at[h, p, t], send_sem=sends.at[SWAP],
            recv_sem=own_recv.at[t if i == 0 else 2], device_id={"blk": nb}, device_id_type=MESH,
        )

    def hand(panel, u):
        return pltpu.make_async_remote_copy(
            src_ref=stage.at[panel, u], dst_ref=landed.at[panel, u],
            send_sem=sends.at[HAND], recv_sem=res_recv.at[panel // 2, u],
            device_id={"blk": nb}, device_id_type=MESH,
        )

    def gram(p, side):
        total = None
        for h in range(2):
            for a in range(2):
                left = own[h, p, :, a].reshape(per * tile, -1)
                right = side(h, 1 - a).reshape(-1, own.shape[5])
                part = lax.dot_general(
                    left, right, (((1,), (1,)), ((), ())), preferred_element_type=jnp.float32
                )
                total = part if total is None else total + part
        return total * scale

    def finish(p, panel, u, part, diagonal=False):
        for t in range(per):
            slot = panel * per + u
            weight = held[t, p, slot]
            half = part(t) + RIDGE * weight
            if diagonal and t == u:
                rows = lax.broadcasted_iota(jnp.int32, (tile, tile), 0)
                columns = lax.broadcasted_iota(jnp.int32, (tile, tile), 1)
                on_diag = rows == columns + b * (2 * tile)
                inverse = jnp.where(on_diag, 1.0 / jnp.where(on_diag, weight, 1.0), 0.0)
                stepped = weight - STEP * (half - inverse)
            else:
                stepped = weight - STEP * half
            bound = STEP * LASSO
            updated = stepped - jnp.clip(stepped, -bound, bound)
            if diagonal and t == u:
                updated = jnp.where(on_diag, stepped, updated)
            flag = flags[2 * t + p, slot].astype(jnp.float32)
            held[t, p, slot] = updated * flag

    def cut(total, u=0):
        return lambda t: total[t * tile:(t + 1) * tile, u * tile:(u + 1) * tile]

    def finish_all(p, panel, total, diagonal=False):
        for u in range(per):
            finish(p, panel, u, cut(total, u), diagonal)

    def keep(panel):
        total = gram(0, lambda h, a: cols[h, panel, :, a])
        finish_all(0, panel, total)
        return total

    def emit(across, d, p, u, part):
        t = per - 1
        out[across, d, p, u, t] = part(t).T

        @pl.when(across == 1)
        def _():
            via(d, p, u).start()

        @pl.when(jnp.where(across == 0, nb, -1) == p)
        def _():
            for t in range(per - 1):
                out[0, d, p, u, t] = part(t).T

    def pass_on(h, step):
        arrive(h, step[2], step[0])
        start(step_pushes(h, step))

    def forward(n):
        step = decode(n)
        for h in (b, nb):
            pass_on(h, step)

    pltpu.make_async_copy(own.at[b], own.at[b], fill.at[0]).wait()
    for i in range(2):
        for t in range(per):
            swap(b, i, t).start()
    for t in range(per):
        start(own_pushes(b, t))
    load_weights.start()
    start(beside_push(b))
    for t in range(per):
        swap(nb, 0, t).wait_recv()
        start(own_pushes(nb, t))

    def early(n, carry):
        forward(n)
        return carry

    lax.fori_loop(0, ahead, early, 0)
    took(own.at[nb, nb], own_recv.at[2])
    start(beside_push(nb))
    load_weights.wait()

    def receive(n):
        step = decode(n)
        u, handed, across, served = step[2], step[5], step[7], step[8]

        @pl.when(handed == 1)
        def _():
            chip = step[0] // 2
            took(landed.at[pl.ds(2 * chip, 2), u], res_recv.at[chip, u])
            for d in range(2):
                panel = step[d]
                finish(1, panel, u, lambda t: landed[panel, u, t])

                @pl.when(served == 1)
                def _():
                    emit(across, d, 1, u, lambda t: landed[panel, u, t])

    def settle(n, carry):
        receive(n)
        return carry

    def nearby():
        for p in range(2):
            parity = b if p == 0 else nb
            finish_all(p, w, gram(p, lambda h, a: own[h, parity, :, a]), True)
        for u in range(per):
            arrive_beside(u, c_target)
        took(beside, beside_recv.at[0])
        keep(c_target)
        finish_all(1, c_target, gram(1, lambda h, a: beside[h, :, a]))

    def compute(n, carry):
        f = n + 2 * inner

        @pl.when(jnp.logical_and(f >= ahead, f < count))
        def _():
            forward(f)

        first, second, u, _, _, handed, kept, across, served = decode(n)

        def both(i, carry):
            panel = jnp.where(i == 0, first, second)

            @pl.when(i == 1)
            def _():
                arrive_beside(u, panel)

            @pl.when(handed == 1)
            def _():
                total = cut(gram(1, lambda h, a: cols[h, panel, u, a]))
                for t in range(per):
                    stage[panel, u, t] = total(t)
                hand(panel, u).start()

            @pl.when(kept == 1)
            def _():
                total = keep(panel)

                @pl.when(served == 1)
                def _():
                    for v in range(per):
                        emit(across, i, 0, v, cut(total, v))

            @pl.when(kept == 2)
            def _():
                finish(0, panel, u, cut(gram(0, lambda h, a: cols[h, panel, u, a])))

            return carry

        lax.fori_loop(0, 2, both, 0)

        @pl.when(n == ahead - 1)
        def _():
            nearby()

        @pl.when(n == BATCH)
        def _():
            lax.fori_loop(0, BATCH - LAG, settle, 0)

        @pl.when(n >= BATCH)
        def _():
            receive(n - LAG)

        @pl.when(inner == 1)
        def _():
            @pl.when(n == STEPS - 5)
            def _():
                for h in (b, nb):
                    start(near_own(h, 0))

            @pl.when(n == STEPS - 4)
            def _():
                for u in range(per):
                    for d in range(2):
                        for p in range(2):
                            direct(d, p, u, per - 1).start()
                        for t in range(per - 1):
                            direct(d, nb, u, t).start()

            @pl.when(n == STEPS - 2)
            def _():
                for h in (b, nb):
                    start(near_own(h, 1))
                    start(pair_own(h))
                relay(0)

            @pl.when(n == STEPS - 1)
            def _():
                relay(1)

        return carry

    def relay(k):
        p = min(k, 1)
        tiles = range(per) if k == 0 else (k - 1,)
        took(passing.at[:, p] if k == 0 else passing.at[:, p, k - 1], passing_recv.at[k])
        for u in tiles:
            for d in range(2):
                onward(d, p, u).start()

    lax.fori_loop(0, count, compute, 0)

    @pl.when(inner == 1)
    def _():
        receive(count - LAG)
        near_arrive(0)
        for h in (b, nb):
            start(near_relay(h, 0))
        relay(2)
        lax.fori_loop(count - LAG + 1, count - 2, settle, 0)
        near_arrive(1)
        for h in (b, nb):
            start(near_relay(h, 1))
        pair_arrive(0)
        for h in (b, nb):
            start(pair_relay(h))

        def adjacent(d, carry):
            cc = jnp.where(d == 0, c, 1 - c)

            @pl.when(d == 1)
            def _():
                took(near.at[:, 1], near_recv.at[2])
                pair_arrive(1)

            finish_all(1, at(z, 1 - y, cc), gram(1, lambda h, a: near[h, d, :, a]))
            finish(1, at(inward, y, cc), per - 1, cut(gram(1, lambda h, a: pair[h, d, a])))
            return carry

        lax.fori_loop(0, 2, adjacent, 0)

        sent(got.at[:3, :, :, 0], DIRECT)
        sent(passing, VIA)
        sent(passing, ONWARD)
        sent(near, NEAR)
        sent(pair, PAIR)
        sent(cols.at[0, :11], ALONG)
        sent(cols.at[0, :4], OVER)
        sent(cols.at[:, :8], CORE)

    @pl.when(inner == 0)
    def _():
        def accept(k, t, p):
            d = k % 2
            panel = at(inward, jnp.where(k < 2, y, 1 - y), jnp.where(d == 0, c, 1 - c))
            finish(jnp.where(p == 0, b, nb), panel, t, lambda u: got[k, p, u, t])

        def closer(k, carry):
            for t in range(per - 1):
                accept(k, t, nb)
            for p in range(2):
                accept(k, per - 1, p)
            return carry

        def farther(k, carry):
            accept(k % 2 + 2, per - 1, k // 2)
            return carry

        lax.fori_loop(count - LAG, count - 2, settle, 0)
        took(got.at[:3, :, :, 0], got_recv.at[0])
        lax.fori_loop(0, 2, closer, 0)
        took(got.at[2:, :, :, per - 1], got_recv.at[1])
        lax.fori_loop(0, 4, farther, 0)
        sent(cols.at[0, :4], ALONG)
        sent(cols.at[0, :7], OVER)
        sent(cols.at[:, :7], CORE)

    sent(own.at[b], SWAP)
    sent(beside, BESIDE)
    lax.fori_loop(count - 2, count, settle, 0)
    sent(stage.at[:11], HAND)


def ring(resid, samples, precision, active):
    panels = lax.axis_size("wide")
    row_tiles, _, per_class, tile, _ = precision.shape
    per = row_tiles // 2
    half = resid.shape[1]
    depth = panels // 4
    scale = 0.5 / (2 * half)
    any_spec = pl.BlockSpec(memory_space=pl.ANY)
    bf16, f32 = resid.dtype, jnp.float32
    dma = pltpu.SemaphoreType.DMA
    updated = pl.pallas_call(
        functools.partial(kernel, depth, scale),
        out_shape=pltpu.VMEM((per, 2, per_class, tile, tile), f32),
        in_specs=[any_spec, any_spec, any_spec, pl.BlockSpec(memory_space=pltpu.SMEM)],
        out_specs=pl.BlockSpec(memory_space=pltpu.VMEM),
        scratch_shapes=[
            pltpu.VMEM((2, 2, per, 2, tile, half), bf16),
            pltpu.VMEM((2, panels, per, 2, tile, half), bf16),
            pltpu.VMEM((2, per, 2, tile, half), bf16),
            pltpu.VMEM((2, 2, per, 2, tile, half), bf16),
            pltpu.VMEM((2, 2, 2, tile, half), bf16),
            pltpu.VMEM((panels, per, per, tile, tile), f32),
            pltpu.VMEM((panels, per, per, tile, tile), f32),
            pltpu.VMEM((2, 2, 2, per, per, tile, tile), f32),
            pltpu.VMEM((4, 2, per, per, tile, tile), f32),
            pltpu.VMEM((2, 2, per, tile, tile), f32),
            dma((2, panels // 2, per)),
            dma((panels // 2, per)),
            dma((3,)),
            dma((panels // 2, per)),
            dma((1,)),
            dma((3,)),
            dma((2,)),
            dma((2,)),
            dma((3,)),
            dma((11,)),
            dma((2,)),
        ],
        compiler_params=pltpu.CompilerParams(
            collective_id=0, has_side_effects=True, vmem_limit_bytes=52 * 1024 * 1024
        ),
    )(
        resid.reshape(per, 2, tile, half),
        samples.reshape(per, 2, tile, half),
        precision.reshape(per, 2, per_class, tile, tile),
        active[:, 0],
    )
    return updated.reshape(precision.shape)


def body(resid, samples, precision, active):
    panels = lax.axis_size("wide")
    row_tiles, _, per_class, tile, _ = precision.shape
    words = 8 * per_class * row_tiles * tile * tile + 4 * panels * row_tiles * tile * resid.shape[1]
    if lax.axis_size("blk") == 2 and panels // 4 == 4 and row_tiles == 4 and words < 52 * 1024 * 1024:
        return ring(resid, samples, precision, active)
    return local(resid, samples, precision, active)


def solution(mesh):
    in_specs = (
        P("wide", "blk"),
        P("wide", "blk"),
        P("wide", "blk", None, None, None),
        P("wide", "blk", None),
    )
    out_specs = P("wide", "blk", None, None, None)
    return jax.shard_map(body, mesh=mesh, in_specs=in_specs, out_specs=out_specs, check_vma=False)
```

```python
import functools

import jax
import jax.numpy as jnp
from jax import lax
from jax.experimental import pallas as pl
from jax.experimental.pallas import tpu as pltpu
from jax.sharding import PartitionSpec as P

STEP = 1.0
LASSO = 0.1
RIDGE = 0.5


def local(resid, samples, precision, active):
    groups = lax.axis_size("blk")
    column_group = lax.axis_index("blk")
    panel_index = lax.axis_index("wide")
    row_tiles = precision.shape[0]
    per_class = precision.shape[2]
    tile_size = precision.shape[3]
    tiles = per_class * groups
    local_samples = resid.shape[1]
    total_samples = local_samples * groups
    own_rows = panel_index * row_tiles + jnp.arange(row_tiles, dtype=jnp.int32)
    first_column = (column_group - own_rows) % groups
    own_resid = resid.reshape(row_tiles, tile_size, local_samples)
    own_data = samples.reshape(row_tiles, tile_size, local_samples)
    all_resid, all_data = (
        lax.all_gather(resid, "wide", axis=0, tiled=True),
        lax.all_gather(samples, "wide", axis=0, tiled=True),
    )
    resid_tiles = all_resid.reshape(tiles, tile_size, local_samples)
    data_tiles = all_data.reshape(tiles, tile_size, local_samples)
    positions = jnp.arange(per_class * lax.axis_size("blk"), dtype=jnp.int32)
    classes = positions // per_class
    within = positions % per_class
    column_ids = (classes[:, None] - own_rows[None, :]) % groups + groups * within[:, None]
    forward = jnp.einsum(
        "kis,pkjs->pkij", own_resid, data_tiles[column_ids], preferred_element_type=jnp.float32
    )
    backward = jnp.einsum(
        "kis,pkjs->pkij", own_data, resid_tiles[column_ids], preferred_element_type=jnp.float32
    )
    summed = (
        lax.psum_scatter(0.5 * (forward + backward), "blk", scatter_dimension=0, tiled=True)
        / total_samples
    )
    precision_tiles = precision[:, 0]
    active_flags = active[:, 0].astype(jnp.float32)
    gradient_part = summed.transpose(1, 0, 2, 3)
    column_ids = first_column[:, None] + groups * jnp.arange(per_class, dtype=jnp.int32)[None, :]
    same_tile = column_ids == own_rows[:, None]
    identity = jnp.eye(tile_size, dtype=bool)
    on_diag = same_tile[:, :, None, None] & identity
    inverse = jnp.where(on_diag, 1.0 / jnp.where(on_diag, precision_tiles, 1.0), 0.0)
    stepped = precision_tiles - STEP * (gradient_part + RIDGE * precision_tiles - inverse)
    shrunk = jnp.sign(stepped) * jnp.maximum(jnp.abs(stepped) - STEP * LASSO, 0.0)
    updated = jnp.where(on_diag, stepped, shrunk) * active_flags[:, :, None, None]
    return updated[:, None]


MESH = pl.DeviceIdType.MESH

END = (
    (0, 1, 0, 1, 0, 3, 0), (1, 0, 0, 0, 1, 2, 2), (0, 1, 1, 1, 0, 3, 1), (2, 0, 0, 0, 1, 1, 0),
    (2, 0, 1, 0, 1, 1, 1), (1, 1, 0, 0, 0, 1, 2), (3, 0, 0, 0, 1, 1, 0), (2, 1, 0, 0, 0, 1, 0),
    (3, 0, 1, 0, 1, 1, 1), (2, 1, 1, 0, 0, 1, 1), (3, 1, 0, 0, 0, 1, 0), (3, 1, 1, 0, 0, 1, 1),
)
INNER = (
    (2, 0, 0, 2, 1, 1, 0), (0, 0, 0, 1, 0, 1, 0), (1, 1, 0, 0, 0, 0, 0), (2, 0, 1, 2, 1, 0, 1),
    (0, 0, 1, 1, 0, 1, 1), (1, 1, 1, 0, 0, 0, 1), (3, 0, 0, 2, 0, 1, 0), (0, 1, 0, 1, 0, 1, 0),
    (2, 1, 0, 0, 0, 1, 0), (3, 0, 1, 2, 0, 1, 1), (0, 1, 1, 1, 0, 1, 1), (2, 1, 1, 0, 0, 1, 1),
    (3, 1, 0, 0, 0, 1, 0), (3, 1, 1, 0, 0, 1, 1),
)
STEPS = len(INNER)
EARLY = (3, 6)
LAG = 3
BATCH = 8
ALONG, OVER, CORE, HAND, SWAP, BESIDE, NEAR, PAIR, DIRECT, VIA, ONWARD, SHARE = range(12)


def packed(row):
    place, across, u, along, over, handed, kept = row
    return place + 4 * across + 8 * u + 16 * along + 64 * over + 128 * handed + 512 * kept


def kernel(
    depth, scale, resid, samples, weights, flags, held,
    own, cols, beside, near, pair, stage, landed, out, got, passing, shared, recv, beside_cols, own_recv,
    res_recv, beside_recv, near_recv, pair_recv, got_recv, passing_recv, sends, fill,
):
    b = lax.axis_index("blk")
    w = lax.axis_index("wide")
    nb = 1 - b
    z, y, c = w // 4, (w // 2) % 2, w % 2
    per = own.shape[2]
    tile = own.shape[4]
    last = depth - 1
    half = z // 2
    inner = jnp.where(z == 0, 0, jnp.where(z == last, 0, 1))
    inward = z + 1 - 2 * half
    outward = jnp.where(inner == 1, z - 1 + 2 * half, inward)

    def at(zz, yy, cc):
        return (zz * 2 + yy) * 2 + cc

    in_target, out_target = at(inward, y, c), at(outward, y, c)
    y_target, c_target = at(z, 1 - y, c), at(z, y, 1 - c)
    count = len(END) + (len(INNER) - len(END)) * inner
    ahead = EARLY[0] + (EARLY[1] - EARLY[0]) * inner

    def decode(n):
        end, mid = jnp.int32(packed(END[0])), jnp.int32(packed(INNER[0]))
        for k in range(1, STEPS):
            if k < len(END):
                end = jnp.where(n == k, jnp.int32(packed(END[k])), end)
            mid = jnp.where(n == k, jnp.int32(packed(INNER[k])), mid)
        code = jnp.where(inner == 1, mid, end)
        place = code % 4
        zz = jnp.where(half == 0, place, last - place)
        across = (code // 4) % 2
        yy = jnp.where(across == 1, 1 - y, y)
        u = (code // 8) % 2
        along = (code // 16) % 4
        over = (code // 64) % 2
        handed = (code // 128) % 4
        kept = code // 512
        served = jnp.where(place == 0, inner, 0)
        return at(zz, yy, c), at(zz, yy, 1 - c), u, along, over, handed, kept, across, served

    loads = []
    for a, src in enumerate((resid, samples)):
        for p in range(2):
            loads.append(
                pltpu.make_async_copy(src.at[:, p], own.at[b, p, :, a], fill.at[0])
            )
    for load in loads:
        load.start()
    load_weights = pltpu.make_async_copy(weights, held, fill.at[1])

    barrier = pltpu.get_barrier_semaphore()

    def greet(**device):
        pl.semaphore_signal(barrier, inc=1, device_id=device, device_id_type=MESH)

    greet(blk=nb)
    greet(wide=y_target)
    greet(wide=c_target)
    greet(wide=in_target)

    @pl.when(inner == 1)
    def _():
        greet(wide=out_target)

    greet(wide=at(outward, y, 1 - c))
    greet(wide=at(z, 1 - y, 1 - c))
    pl.semaphore_wait(barrier, 6 + inner)

    def whole(ref, sent_sem, took_sem):
        return pltpu.make_async_remote_copy(
            src_ref=ref, dst_ref=ref, send_sem=sent_sem, recv_sem=took_sem,
            device_id={"wide": y_target}, device_id_type=MESH,
        )

    def took(ref, sem):
        whole(ref, sends.at[0], sem).wait_recv()

    def sent(ref, k):
        whole(ref, sends.at[k], recv.at[0, 0, 0]).wait_send()

    def push(h, u, src, panel, lane, target):
        sem = beside_cols.at[panel // 2, u] if lane == CORE else recv.at[h, panel // 2, u]
        return pltpu.make_async_remote_copy(
            src_ref=src, dst_ref=cols.at[h, panel, u], send_sem=sends.at[lane],
            recv_sem=sem, device_id={"wide": target}, device_id_type=MESH,
        )

    def arrive(h, u, panel):
        took(cols.at[h, panel, u], recv.at[h, panel // 2, u])

    def arrive_beside(u, panel):
        took(cols.at[:, panel, u], beside_cols.at[panel // 2, u])

    def own_pushes(h, u):
        src = own.at[h, b, u]
        return (
            (None, push(h, u, src, w, OVER, y_target)),
            (None, push(h, u, src, w, ALONG, in_target)),
            (None, push(h, u, src, w, CORE, c_target)),
        ) + (((inner == 1, push(h, u, src, w, ALONG, out_target)),) if u == 0 else ())

    def step_pushes(h, step):
        panel, _, u, along, over = step[:5]
        src = cols.at[h, panel, u]
        target = jnp.where(along == 1, in_target, out_target)
        return (
            (along > 0, push(h, u, src, panel, ALONG, target)),
            (over == 1, push(h, u, src, panel, OVER, y_target)),
            (None, push(h, u, src, panel, CORE, c_target)),
        )

    def beside_push(h):
        return ((None, pltpu.make_async_remote_copy(
            src_ref=own.at[h, nb], dst_ref=beside.at[h], send_sem=sends.at[BESIDE],
            recv_sem=beside_recv.at[0], device_id={"wide": c_target}, device_id_type=MESH,
        )),)

    def near_push(h, d, u, src, target):
        return ((None, pltpu.make_async_remote_copy(
            src_ref=src, dst_ref=near.at[h, d, u], send_sem=sends.at[NEAR],
            recv_sem=near_recv.at[u if d == 0 else 2], device_id={"wide": target}, device_id_type=MESH,
        )),)

    def near_own(h, u):
        return near_push(h, 0, u, own.at[h, nb, u], y_target)

    def near_relay(h, u):
        return near_push(h, 1, u, near.at[h, 0, u], c_target)

    def near_arrive(u):
        took(near.at[:, 0, u], near_recv.at[u])

    def pair_push(h, d, src, target):
        return ((None, pltpu.make_async_remote_copy(
            src_ref=src, dst_ref=pair.at[h, d], send_sem=sends.at[PAIR],
            recv_sem=pair_recv.at[d], device_id={"wide": target}, device_id_type=MESH,
        )),)

    def pair_own(h):
        return pair_push(h, 0, own.at[h, nb, per - 1], in_target)

    def pair_relay(h):
        return pair_push(h, 1, pair.at[h, 0], c_target)

    def pair_arrive(d):
        took(pair.at[:, d], pair_recv.at[d])

    def share():
        return pltpu.make_async_remote_copy(
            src_ref=shared.at[0], dst_ref=shared.at[1], send_sem=sends.at[SHARE],
            recv_sem=got_recv.at[2], device_id={"wide": at(z, 1 - y, jnp.where(y == 0, c, 1 - c))},
            device_id_type=MESH,
        )

    def hands(handed, d):
        alone = jnp.where(handed == 2, 1, jnp.where(handed == 3, y, -1))
        return jnp.logical_or(handed == 1, alone == d)

    def outward_core(d):
        return at(outward, y, jnp.where(d == 0, c, 1 - c))

    def direct(d, p, u, t):
        return pltpu.make_async_remote_copy(
            src_ref=out.at[0, d, p, u, t], dst_ref=got.at[d, p, u, t],
            send_sem=sends.at[DIRECT], recv_sem=got_recv.at[0],
            device_id={"wide": outward_core(d)}, device_id_type=MESH,
        )

    def via(d, p, u):
        return pltpu.make_async_remote_copy(
            src_ref=out.at[1, d, p, u, per - 1], dst_ref=passing.at[d, p, u],
            send_sem=sends.at[VIA], recv_sem=passing_recv.at[p * (1 + u)],
            device_id={"wide": y_target}, device_id_type=MESH,
        )

    def onward(d, p, u):
        return pltpu.make_async_remote_copy(
            src_ref=passing.at[d, p, u], dst_ref=got.at[2 + d, p, u, per - 1],
            send_sem=sends.at[ONWARD], recv_sem=got_recv.at[1],
            device_id={"wide": outward_core(d)}, device_id_type=MESH,
        )

    def start(pushes):
        for when, copy in pushes:
            if when is None:
                copy.start()
            else:
                pl.when(when)(copy.start)

    def swap(h, i, t):
        p = (nb, b)[i] if h is b else (b, nb)[i]
        return pltpu.make_async_remote_copy(
            src_ref=own.at[h, p, t], dst_ref=own.at[h, p, t], send_sem=sends.at[SWAP],
            recv_sem=own_recv.at[t if i == 0 else 2], device_id={"blk": nb}, device_id_type=MESH,
        )

    def hand(panel, u):
        return pltpu.make_async_remote_copy(
            src_ref=stage.at[panel, u], dst_ref=landed.at[panel, u],
            send_sem=sends.at[HAND], recv_sem=res_recv.at[panel // 2, u],
            device_id={"blk": nb}, device_id_type=MESH,
        )

    def gram(p, side):
        total = None
        for h in range(2):
            for a in range(2):
                left = own[h, p, :, a].reshape(per * tile, -1)
                right = side(h, 1 - a).reshape(-1, own.shape[5])
                part = lax.dot_general(
                    left, right, (((1,), (1,)), ((), ())), preferred_element_type=jnp.float32
                )
                total = part if total is None else total + part
        return total * scale

    def finish(p, panel, u, part, diagonal=False):
        for t in range(per):
            slot = panel * per + u
            weight = held[t, p, slot]
            half = part(t) + RIDGE * weight
            if diagonal and t == u:
                rows = lax.broadcasted_iota(jnp.int32, (tile, tile), 0)
                columns = lax.broadcasted_iota(jnp.int32, (tile, tile), 1)
                on_diag = rows == columns + b * (2 * tile)
                inverse = jnp.where(on_diag, 1.0 / jnp.where(on_diag, weight, 1.0), 0.0)
                stepped = weight - STEP * (half - inverse)
            else:
                stepped = weight - STEP * half
            bound = STEP * LASSO
            updated = stepped - jnp.clip(stepped, -bound, bound)
            if diagonal and t == u:
                updated = jnp.where(on_diag, stepped, updated)
            flag = flags[2 * t + p, slot].astype(jnp.float32)
            held[t, p, slot] = updated * flag

    def cut(total, u=0):
        return lambda t: total[t * tile:(t + 1) * tile, u * tile:(u + 1) * tile]

    def finish_all(p, panel, total, diagonal=False):
        for u in range(per):
            finish(p, panel, u, cut(total, u), diagonal)

    def keep(panel):
        total = gram(0, lambda h, a: cols[h, panel, :, a])
        finish_all(0, panel, total)
        return total

    def emit(across, d, p, u, part):
        t = per - 1
        out[across, d, p, u, t] = part(t).T

        @pl.when(across == 1)
        def _():
            via(d, p, u).start()

        @pl.when(jnp.where(across + d == 0, nb, -1) == p)
        def _():
            for t in range(per - 1):
                out[0, d, p, u, t] = part(t).T

    def pass_on(h, step):
        arrive(h, step[2], step[0])
        start(step_pushes(h, step))

    def forward(n):
        step = decode(n)
        for h in (b, nb):
            pass_on(h, step)

    pltpu.make_async_copy(own.at[b], own.at[b], fill.at[0]).wait()
    for i in range(2):
        for t in range(per):
            swap(b, i, t).start()
    for t in range(per):
        start(own_pushes(b, t))
    load_weights.start()
    start(beside_push(b))
    for t in range(per):
        swap(nb, 0, t).wait_recv()
        start(own_pushes(nb, t))

    def early(n, carry):
        forward(n)
        return carry

    lax.fori_loop(0, ahead, early, 0)
    took(own.at[nb, nb], own_recv.at[2])
    start(beside_push(nb))
    load_weights.wait()

    def receive(n):
        step = decode(n)
        u, handed, across, served = step[2], step[5], step[7], step[8]

        chip = step[0] // 2

        @pl.when(handed == 1)
        def _():
            took(landed.at[pl.ds(2 * chip, 2), u], res_recv.at[chip, u])

        @pl.when(handed > 1)
        def _():
            took(landed.at[0, u], res_recv.at[chip, u])

        for d in range(2):
            panel = step[d]

            @pl.when(hands(handed, d))
            def _():
                finish(1, panel, u, lambda t: landed[panel, u, t])

                @pl.when(served == 1)
                def _():
                    emit(across, d, 1, u, lambda t: landed[panel, u, t])

                @pl.when(jnp.where(handed == 3, nb, 0) == 1)
                def _():
                    for t in range(per):
                        shared[0, t, u] = landed[panel, u, t].T

    def settle(n, carry):
        receive(n)
        return carry

    def nearby():
        for p in range(2):
            parity = b if p == 0 else nb
            finish_all(p, w, gram(p, lambda h, a: own[h, parity, :, a]), True)
        for u in range(per):
            arrive_beside(u, c_target)
        took(beside, beside_recv.at[0])
        keep(c_target)
        finish_all(1, c_target, gram(1, lambda h, a: beside[h, :, a]))

    def compute(n, carry):
        f = n + 2 * inner

        @pl.when(jnp.logical_and(f >= ahead, f < count))
        def _():
            forward(f)

        first, second, u, _, _, handed, kept, across, served = decode(n)

        def both(i, carry):
            panel = jnp.where(i == 0, first, second)

            @pl.when(i == 1)
            def _():
                arrive_beside(u, panel)

            @pl.when(hands(handed, i))
            def _():
                total = cut(gram(1, lambda h, a: cols[h, panel, u, a]))
                for t in range(per):
                    stage[panel, u, t] = total(t)
                hand(panel, u).start()

            @pl.when(kept == 1)
            def _():
                total = keep(panel)

                @pl.when(served == 1)
                def _():
                    for v in range(per):
                        emit(across, i, 0, v, cut(total, v))

                @pl.when(jnp.where(handed == 3, nb + jnp.where(i == y, 0, 1), 1) == 0)
                def _():
                    for v in range(per):
                        for t in range(per):
                            shared[0, t, v] = cut(total, v)(t).T

            @pl.when(kept == 2)
            def _():
                finish(0, panel, u, cut(gram(0, lambda h, a: cols[h, panel, u, a])))

            return carry

        lax.fori_loop(0, 2, both, 0)

        @pl.when(n == ahead - 1)
        def _():
            nearby()

        @pl.when(n == BATCH)
        def _():
            lax.fori_loop(0, BATCH - LAG, settle, 0)

        @pl.when(n >= BATCH)
        def _():
            receive(n - LAG)

        @pl.when(jnp.where(inner == 0, n, -1) == BATCH)
        def _():
            share().start()

        @pl.when(inner == 1)
        def _():
            @pl.when(n == STEPS - 9)
            def _():
                for h in (b, nb):
                    start(near_own(h, 0))

            @pl.when(n == STEPS - 7)
            def _():
                for h in (b, nb):
                    start(near_own(h, 1))

            @pl.when(n == STEPS - 4)
            def _():
                for u in range(per):
                    for d in range(2):
                        for p in range(2):
                            direct(d, p, u, per - 1).start()
                    for t in range(per - 1):
                        direct(0, nb, u, t).start()

            @pl.when(n == STEPS - 2)
            def _():
                for h in (b, nb):
                    start(pair_own(h))
                relay(0)

            @pl.when(n == STEPS - 1)
            def _():
                relay(1)

        return carry

    def relay(k):
        p = min(k, 1)
        tiles = range(per) if k == 0 else (k - 1,)
        took(passing.at[:, p] if k == 0 else passing.at[:, p, k - 1], passing_recv.at[k])
        for u in tiles:
            for d in range(2):
                onward(d, p, u).start()

    lax.fori_loop(0, count, compute, 0)

    @pl.when(inner == 1)
    def _():
        receive(count - LAG)
        near_arrive(0)
        for h in (b, nb):
            start(near_relay(h, 0))
        relay(2)
        lax.fori_loop(count - LAG + 1, count - 2, settle, 0)
        near_arrive(1)
        for h in (b, nb):
            start(near_relay(h, 1))
        pair_arrive(0)
        for h in (b, nb):
            start(pair_relay(h))

        def adjacent(d, carry):
            cc = jnp.where(d == 0, c, 1 - c)

            @pl.when(d == 1)
            def _():
                took(near.at[:, 1], near_recv.at[2])
                pair_arrive(1)

            finish_all(1, at(z, 1 - y, cc), gram(1, lambda h, a: near[h, d, :, a]))
            finish(1, at(inward, y, cc), per - 1, cut(gram(1, lambda h, a: pair[h, d, a])))
            return carry

        lax.fori_loop(0, 2, adjacent, 0)

        sent(held.at[:, 0, :5], DIRECT)
        sent(passing, VIA)
        sent(passing, ONWARD)
        sent(near, NEAR)
        sent(pair, PAIR)
        sent(cols.at[0, :11], ALONG)
        sent(cols.at[0, :4], OVER)
        sent(cols.at[:, :8], CORE)

    @pl.when(inner == 0)
    def _():
        def accept(k, t, p):
            d = k % 2
            panel = at(inward, jnp.where(k < 2, y, 1 - y), jnp.where(d == 0, c, 1 - c))
            finish(jnp.where(p == 0, b, nb), panel, t, lambda u: got[k, p, u, t])

        def closer(k, carry):
            @pl.when(k == 0)
            def _():
                for t in range(per - 1):
                    accept(k, t, nb)

            for p in range(2):
                accept(k, per - 1, p)
            return carry

        def farther(k, carry):
            accept(k % 2 + 2, per - 1, k // 2)
            return carry

        lax.fori_loop(count - LAG, count - 2, settle, 0)
        took(held.at[:, 0, :5], got_recv.at[0])
        lax.fori_loop(0, 2, closer, 0)
        took(got.at[2:, :, :, per - 1], got_recv.at[1])
        lax.fori_loop(0, 4, farther, 0)
        sent(cols.at[0, :4], ALONG)
        sent(cols.at[0, :7], OVER)
        sent(cols.at[:, :7], CORE)
        took(shared.at[1], got_recv.at[2])
        for t in range(per):
            finish(1, at(z, 1 - y, jnp.where(y == 1, c, 1 - c)), t, lambda u: shared[1, t, u])
        sent(shared.at[0], SHARE)

    sent(own.at[b], SWAP)
    sent(beside, BESIDE)
    lax.fori_loop(count - 2, count, settle, 0)

    @pl.when(inner == 0)
    def _():
        sent(held.at[:, 0, :21], HAND)

    @pl.when(inner == 1)
    def _():
        sent(held.at[:, 0, :22], HAND)


def ring(resid, samples, precision, active):
    panels = lax.axis_size("wide")
    row_tiles, _, per_class, tile, _ = precision.shape
    per = row_tiles // 2
    half = resid.shape[1]
    depth = panels // 4
    scale = 0.5 / (2 * half)
    any_spec = pl.BlockSpec(memory_space=pl.ANY)
    bf16, f32 = resid.dtype, jnp.float32
    dma = pltpu.SemaphoreType.DMA
    updated = pl.pallas_call(
        functools.partial(kernel, depth, scale),
        out_shape=pltpu.VMEM((per, 2, per_class, tile, tile), f32),
        in_specs=[any_spec, any_spec, any_spec, pl.BlockSpec(memory_space=pltpu.SMEM)],
        out_specs=pl.BlockSpec(memory_space=pltpu.VMEM),
        scratch_shapes=[
            pltpu.VMEM((2, 2, per, 2, tile, half), bf16),
            pltpu.VMEM((2, panels, per, 2, tile, half), bf16),
            pltpu.VMEM((2, per, 2, tile, half), bf16),
            pltpu.VMEM((2, 2, per, 2, tile, half), bf16),
            pltpu.VMEM((2, 2, 2, tile, half), bf16),
            pltpu.VMEM((panels, per, per, tile, tile), f32),
            pltpu.VMEM((panels, per, per, tile, tile), f32),
            pltpu.VMEM((2, 2, 2, per, per, tile, tile), f32),
            pltpu.VMEM((4, 2, per, per, tile, tile), f32),
            pltpu.VMEM((2, 2, per, tile, tile), f32),
            pltpu.VMEM((2, per, per, tile, tile), f32),
            dma((2, panels // 2, per)),
            dma((panels // 2, per)),
            dma((3,)),
            dma((panels // 2, per)),
            dma((1,)),
            dma((3,)),
            dma((2,)),
            dma((3,)),
            dma((3,)),
            dma((12,)),
            dma((2,)),
        ],
        compiler_params=pltpu.CompilerParams(
            collective_id=0, has_side_effects=True, vmem_limit_bytes=52 * 1024 * 1024
        ),
    )(
        resid.reshape(per, 2, tile, half),
        samples.reshape(per, 2, tile, half),
        precision.reshape(per, 2, per_class, tile, tile),
        active[:, 0],
    )
    return updated.reshape(precision.shape)


def body(resid, samples, precision, active):
    panels = lax.axis_size("wide")
    row_tiles, _, per_class, tile, _ = precision.shape
    words = 8 * per_class * row_tiles * tile * tile + 4 * panels * row_tiles * tile * resid.shape[1]
    if lax.axis_size("blk") == 2 and panels // 4 == 4 and row_tiles == 4 and words < 52 * 1024 * 1024:
        return ring(resid, samples, precision, active)
    return local(resid, samples, precision, active)


def solution(mesh):
    in_specs = (
        P("wide", "blk"),
        P("wide", "blk"),
        P("wide", "blk", None, None, None),
        P("wide", "blk", None),
    )
    out_specs = P("wide", "blk", None, None, None)
    return jax.shard_map(body, mesh=mesh, in_specs=in_specs, out_specs=out_specs, check_vma=False)
```

```python
import functools

import jax
import jax.numpy as jnp
from jax import lax
from jax.experimental import pallas as pl
from jax.experimental.pallas import tpu as pltpu
from jax.sharding import PartitionSpec as P

STEP = 1.0
LASSO = 0.1
RIDGE = 0.5


def local(resid, samples, precision, active):
    groups = lax.axis_size("blk")
    column_group = lax.axis_index("blk")
    panel_index = lax.axis_index("wide")
    row_tiles = precision.shape[0]
    per_class = precision.shape[2]
    tile_size = precision.shape[3]
    tiles = per_class * groups
    local_samples = resid.shape[1]
    total_samples = local_samples * groups
    own_rows = panel_index * row_tiles + jnp.arange(row_tiles, dtype=jnp.int32)
    first_column = (column_group - own_rows) % groups
    own_resid = resid.reshape(row_tiles, tile_size, local_samples)
    own_data = samples.reshape(row_tiles, tile_size, local_samples)
    all_resid, all_data = (
        lax.all_gather(resid, "wide", axis=0, tiled=True),
        lax.all_gather(samples, "wide", axis=0, tiled=True),
    )
    resid_tiles = all_resid.reshape(tiles, tile_size, local_samples)
    data_tiles = all_data.reshape(tiles, tile_size, local_samples)
    positions = jnp.arange(per_class * lax.axis_size("blk"), dtype=jnp.int32)
    classes = positions // per_class
    within = positions % per_class
    column_ids = (classes[:, None] - own_rows[None, :]) % groups + groups * within[:, None]
    forward = jnp.einsum(
        "kis,pkjs->pkij", own_resid, data_tiles[column_ids], preferred_element_type=jnp.float32
    )
    backward = jnp.einsum(
        "kis,pkjs->pkij", own_data, resid_tiles[column_ids], preferred_element_type=jnp.float32
    )
    summed = (
        lax.psum_scatter(0.5 * (forward + backward), "blk", scatter_dimension=0, tiled=True)
        / total_samples
    )
    precision_tiles = precision[:, 0]
    active_flags = active[:, 0].astype(jnp.float32)
    gradient_part = summed.transpose(1, 0, 2, 3)
    column_ids = first_column[:, None] + groups * jnp.arange(per_class, dtype=jnp.int32)[None, :]
    same_tile = column_ids == own_rows[:, None]
    identity = jnp.eye(tile_size, dtype=bool)
    on_diag = same_tile[:, :, None, None] & identity
    inverse = jnp.where(on_diag, 1.0 / jnp.where(on_diag, precision_tiles, 1.0), 0.0)
    stepped = precision_tiles - STEP * (gradient_part + RIDGE * precision_tiles - inverse)
    shrunk = jnp.sign(stepped) * jnp.maximum(jnp.abs(stepped) - STEP * LASSO, 0.0)
    updated = jnp.where(on_diag, stepped, shrunk) * active_flags[:, :, None, None]
    return updated[:, None]


MESH = pl.DeviceIdType.MESH

END = (
    (0, 1, 0, 1, 0, 3, 0), (1, 0, 0, 0, 1, 2, 2), (0, 1, 1, 1, 0, 3, 1), (2, 0, 0, 0, 1, 1, 0),
    (2, 0, 1, 0, 1, 1, 1), (1, 1, 0, 0, 0, 1, 2), (3, 0, 0, 0, 1, 1, 0), (2, 1, 0, 0, 0, 1, 0),
    (3, 0, 1, 0, 2, 1, 1), (2, 1, 1, 0, 0, 1, 1), (3, 1, 0, 0, 0, 1, 0), (3, 1, 1, 3, 0, 1, 1),
)
INNER = (
    (2, 0, 0, 2, 1, 1, 0), (0, 0, 0, 1, 0, 1, 0), (1, 1, 0, 0, 0, 0, 0), (2, 0, 1, 2, 1, 0, 1),
    (0, 0, 1, 1, 0, 0, 1), (1, 1, 1, 0, 0, 0, 1), (3, 0, 0, 2, 0, 1, 0), (0, 1, 0, 1, 0, 1, 0),
    (2, 1, 0, 0, 0, 1, 0), (3, 0, 1, 2, 0, 1, 1), (0, 1, 1, 1, 0, 1, 1), (2, 1, 1, 0, 0, 1, 1),
    (3, 1, 0, 0, 0, 1, 0), (3, 1, 1, 0, 0, 1, 1),
)
STEPS = len(INNER)
EARLY = (3, 6)
LAG = 3
BATCH = 8
ALONG, OVER, CORE, HAND, SWAP, BESIDE, NEAR, PAIR, DIRECT, VIA, ONWARD, SHARE, CROSS = range(13)


def packed(row):
    place, across, u, along, over, handed, kept = row
    return place + 4 * across + 8 * u + 16 * along + 64 * over + 256 * handed + 1024 * kept


def kernel(
    depth, scale, resid, samples, weights, flags, held,
    own, cols, beside, near, pair, stage, landed, out, got, passing, shared, crossed, recv, beside_cols, own_recv,
    res_recv, halves, beside_recv, near_recv, pair_recv, got_recv, passing_recv, sends, crossed_recv, fill,
):
    b = lax.axis_index("blk")
    w = lax.axis_index("wide")
    nb = 1 - b
    z, y, c = w // 4, (w // 2) % 2, w % 2
    per = own.shape[2]
    tile = own.shape[4]
    last = depth - 1
    half = z // 2
    inner = jnp.where(z == 0, 0, jnp.where(z == last, 0, 1))
    inward = z + 1 - 2 * half
    outward = jnp.where(inner == 1, z - 1 + 2 * half, inward)

    def at(zz, yy, cc):
        return (zz * 2 + yy) * 2 + cc

    in_target, out_target = at(inward, y, c), at(outward, y, c)
    y_target, c_target = at(z, 1 - y, c), at(z, y, 1 - c)
    count = len(END) + (len(INNER) - len(END)) * inner
    ahead = EARLY[0] + (EARLY[1] - EARLY[0]) * inner

    def decode(n):
        end, mid = jnp.int32(packed(END[0])), jnp.int32(packed(INNER[0]))
        for k in range(1, STEPS):
            if k < len(END):
                end = jnp.where(n == k, jnp.int32(packed(END[k])), end)
            mid = jnp.where(n == k, jnp.int32(packed(INNER[k])), mid)
        code = jnp.where(inner == 1, mid, end)
        place = code % 4
        zz = jnp.where(half == 0, place, last - place)
        across = (code // 4) % 2
        yy = jnp.where(across == 1, 1 - y, y)
        u = (code // 8) % 2
        along = (code // 16) % 4
        over = (code // 64) % 4
        handed = (code // 256) % 4
        kept = code // 1024
        served = jnp.where(place == 0, inner, 0)
        return at(zz, yy, c), at(zz, yy, 1 - c), u, along, over, handed, kept, across, served

    loads = []
    for a, src in enumerate((resid, samples)):
        for p in range(2):
            loads.append(
                pltpu.make_async_copy(src.at[:, p], own.at[b, p, :, a], fill.at[0])
            )
    for load in loads:
        load.start()
    load_weights = pltpu.make_async_copy(weights, held, fill.at[1])

    barrier = pltpu.get_barrier_semaphore()

    def greet(**device):
        pl.semaphore_signal(barrier, inc=1, device_id=device, device_id_type=MESH)

    greet(blk=nb)
    greet(wide=y_target)
    greet(wide=c_target)
    greet(wide=in_target)

    @pl.when(inner == 1)
    def _():
        greet(wide=out_target)

    greet(wide=at(outward, y, 1 - c))
    greet(wide=at(z, 1 - y, 1 - c))
    pl.semaphore_wait(barrier, 6 + inner)

    def whole(ref, sent_sem, took_sem):
        return pltpu.make_async_remote_copy(
            src_ref=ref, dst_ref=ref, send_sem=sent_sem, recv_sem=took_sem,
            device_id={"wide": y_target}, device_id_type=MESH,
        )

    def took(ref, sem):
        whole(ref, sends.at[0], sem).wait_recv()

    def sent(ref, k):
        whole(ref, sends.at[k], recv.at[0, 0, 0]).wait_send()

    def push(h, u, src, panel, lane, target):
        sem = beside_cols.at[panel // 2, u] if lane == CORE else recv.at[h, panel // 2, u]
        return pltpu.make_async_remote_copy(
            src_ref=src, dst_ref=cols.at[h, panel, u], send_sem=sends.at[lane],
            recv_sem=sem, device_id={"wide": target}, device_id_type=MESH,
        )

    def arrive(h, u, panel):
        took(cols.at[h, panel, u], recv.at[h, panel // 2, u])

    def arrive_beside(u, panel):
        took(cols.at[:, panel, u], beside_cols.at[panel // 2, u])

    def own_pushes(h, u):
        src = own.at[h, b, u]
        return (
            (None, push(h, u, src, w, OVER, y_target)),
            (None, push(h, u, src, w, ALONG, in_target)),
            (None, push(h, u, src, w, CORE, c_target)),
        ) + (((inner == 1, push(h, u, src, w, ALONG, out_target)),) if u == 0 else ())

    def step_pushes(h, step):
        panel, _, u, along, over = step[:5]
        src = cols.at[h, panel, u]
        target = jnp.where(along == 1, in_target, out_target)
        return (
            (along % 3 > 0, push(h, u, src, panel, ALONG, target)),
            (over == 1, push(h, u, src, panel, OVER, y_target)),
            (None, push(h, u, src, panel, CORE, c_target)),
        )

    def beside_push(h):
        return ((None, pltpu.make_async_remote_copy(
            src_ref=own.at[h, nb], dst_ref=beside.at[h], send_sem=sends.at[BESIDE],
            recv_sem=beside_recv.at[0], device_id={"wide": c_target}, device_id_type=MESH,
        )),)

    def near_push(h, d, u, src, target):
        return ((None, pltpu.make_async_remote_copy(
            src_ref=src, dst_ref=near.at[h, d, u], send_sem=sends.at[NEAR],
            recv_sem=near_recv.at[u if d == 0 else 2], device_id={"wide": target}, device_id_type=MESH,
        )),)

    def near_own(h, u):
        return near_push(h, 0, u, own.at[h, nb, u], y_target)

    def near_relay(h, u):
        return near_push(h, 1, u, near.at[h, 0, u], c_target)

    def near_arrive(u):
        took(near.at[:, 0, u], near_recv.at[u])

    def pair_push(h, d, src, target):
        return ((None, pltpu.make_async_remote_copy(
            src_ref=src, dst_ref=pair.at[h, d], send_sem=sends.at[PAIR],
            recv_sem=pair_recv.at[d], device_id={"wide": target}, device_id_type=MESH,
        )),)

    def pair_own(h):
        return pair_push(h, 0, own.at[h, nb, per - 1], in_target)

    def pair_relay(h):
        return pair_push(h, 1, pair.at[h, 0], c_target)

    def pair_arrive(d):
        took(pair.at[:, d], pair_recv.at[d])

    def share():
        return pltpu.make_async_remote_copy(
            src_ref=shared.at[0], dst_ref=shared.at[1], send_sem=sends.at[SHARE],
            recv_sem=got_recv.at[2], device_id={"wide": at(z, 1 - y, jnp.where(y == 0, c, 1 - c))},
            device_id_type=MESH,
        )

    def hands(handed, d):
        alone = jnp.where(handed == 2, 1, jnp.where(handed == 3, y, -1))
        return jnp.logical_or(handed == 1, alone == d)

    def cross(h, d, src, target):
        return pltpu.make_async_remote_copy(
            src_ref=src, dst_ref=crossed.at[h, d], send_sem=sends.at[CROSS],
            recv_sem=crossed_recv.at[d], device_id={"wide": target}, device_id_type=MESH,
        )

    def outward_core(d):
        return at(outward, y, jnp.where(d == 0, c, 1 - c))

    def direct(d, p, u, t):
        return pltpu.make_async_remote_copy(
            src_ref=out.at[0, d, p, u, t], dst_ref=got.at[d, p, u, t],
            send_sem=sends.at[DIRECT], recv_sem=got_recv.at[0],
            device_id={"wide": outward_core(d)}, device_id_type=MESH,
        )

    def via(d, p, u):
        return pltpu.make_async_remote_copy(
            src_ref=out.at[1, d, p, u, per - 1], dst_ref=passing.at[d, p, u],
            send_sem=sends.at[VIA], recv_sem=passing_recv.at[p * (1 + u)],
            device_id={"wide": y_target}, device_id_type=MESH,
        )

    def onward(d, p, u):
        return pltpu.make_async_remote_copy(
            src_ref=passing.at[d, p, u], dst_ref=got.at[2 + d, p, u, per - 1],
            send_sem=sends.at[ONWARD], recv_sem=got_recv.at[1],
            device_id={"wide": outward_core(d)}, device_id_type=MESH,
        )

    def start(pushes):
        for when, copy in pushes:
            if when is None:
                copy.start()
            else:
                pl.when(when)(copy.start)

    def swap(h, i, t):
        p = (nb, b)[i] if h is b else (b, nb)[i]
        return pltpu.make_async_remote_copy(
            src_ref=own.at[h, p, t], dst_ref=own.at[h, p, t], send_sem=sends.at[SWAP],
            recv_sem=own_recv.at[t if i == 0 else 2], device_id={"blk": nb}, device_id_type=MESH,
        )

    def hand(panel, u):
        return pltpu.make_async_remote_copy(
            src_ref=stage.at[panel, u], dst_ref=landed.at[panel, u],
            send_sem=sends.at[HAND], recv_sem=res_recv.at[panel // 2, u],
            device_id={"blk": nb}, device_id_type=MESH,
        )

    def gram(p, side):
        total = None
        for h in range(2):
            for a in range(2):
                left = own[h, p, :, a].reshape(per * tile, -1)
                right = side(h, 1 - a).reshape(-1, own.shape[5])
                part = lax.dot_general(
                    left, right, (((1,), (1,)), ((), ())), preferred_element_type=jnp.float32
                )
                total = part if total is None else total + part
        return total * scale

    def finish(p, panel, u, part, diagonal=False):
        for t in range(per):
            slot = panel * per + u
            weight = held[t, p, slot]
            half = part(t) + RIDGE * weight
            if diagonal and t == u:
                rows = lax.broadcasted_iota(jnp.int32, (tile, tile), 0)
                columns = lax.broadcasted_iota(jnp.int32, (tile, tile), 1)
                on_diag = rows == columns + b * (2 * tile)
                inverse = jnp.where(on_diag, 1.0 / jnp.where(on_diag, weight, 1.0), 0.0)
                stepped = weight - STEP * (half - inverse)
            else:
                stepped = weight - STEP * half
            bound = STEP * LASSO
            updated = stepped - jnp.clip(stepped, -bound, bound)
            if diagonal and t == u:
                updated = jnp.where(on_diag, stepped, updated)
            flag = flags[2 * t + p, slot].astype(jnp.float32)
            held[t, p, slot] = updated * flag

    def cut(total, u=0):
        return lambda t: total[t * tile:(t + 1) * tile, u * tile:(u + 1) * tile]

    def finish_all(p, panel, total, diagonal=False):
        for u in range(per):
            finish(p, panel, u, cut(total, u), diagonal)

    def keep(panel):
        total = gram(0, lambda h, a: cols[h, panel, :, a])
        finish_all(0, panel, total)
        return total

    def emit(across, d, p, u, part):
        t = per - 1
        out[across, d, p, u, t] = part(t).T

        @pl.when(across == 1)
        def _():
            via(d, p, u).start()

        @pl.when(jnp.where(across + d == 0, nb, -1) == p)
        def _():
            for t in range(per - 1):
                out[0, d, p, u, t] = part(t).T

    def pass_on(h, step):
        arrive(h, step[2], step[0])
        start(step_pushes(h, step))

    def piece(ref, h, panel, u, j):
        return ref.at[h, panel, u, :, pl.ds(j * (tile // 2), tile // 2)]

    def half_push(h, panel, u, j, lane, target):
        sem = halves.at[2 + j] if lane == CORE else halves.at[j]
        return pltpu.make_async_remote_copy(
            src_ref=piece(cols, h, panel, u, j), dst_ref=piece(cols, h, panel, u, j),
            send_sem=sends.at[lane], recv_sem=sem, device_id={"wide": target},
            device_id_type=MESH,
        )

    def half_hand(panel, u, j):
        rows = pl.ds(j * (tile // 2), tile // 2)
        return pltpu.make_async_remote_copy(
            src_ref=stage.at[panel, u, :, rows], dst_ref=landed.at[panel, u, :, rows],
            send_sem=sends.at[HAND], recv_sem=res_recv.at[panel // 2, u],
            device_id={"blk": nb}, device_id_type=MESH,
        )

    def by_halves(step):
        u = step[2]
        for j in range(2):
            rows = pl.ds(j * (tile // 2), tile // 2)
            for d in range(2):
                panel = step[d]
                took(cols.at[:, panel, u, :, rows], halves.at[2 * d + j])
                if d == 0:
                    for h in (b, nb):
                        half_push(h, panel, u, j, CORE, c_target).start()
                total = None
                for h in range(2):
                    for a in range(2):
                        part = lax.dot_general(
                            cols[h, panel, u, a, rows],
                            own[h, 1, :, 1 - a].reshape(per * tile, -1),
                            (((1,), (1,)), ((), ())), preferred_element_type=jnp.float32,
                        )
                        total = part if total is None else total + part
                total = total * scale
                for t in range(per):
                    stage[panel, u, t, rows] = total[:, t * tile:(t + 1) * tile]
                half_hand(panel, u, j).start()

    def forward(n):
        step = decode(n)

        @pl.when(step[3] < 3)
        def _():
            for h in (b, nb):
                pass_on(h, step)

        @pl.when(step[4] == 2)
        def _():
            for j in range(2):
                for h in (b, nb):
                    half_push(h, step[0], step[2], j, OVER, y_target).start()

    pltpu.make_async_copy(own.at[b], own.at[b], fill.at[0]).wait()
    for i in range(2):
        for t in range(per):
            swap(b, i, t).start()
    for t in range(per):
        start(own_pushes(b, t))
    load_weights.start()
    start(beside_push(b))
    for t in range(per):
        swap(nb, 0, t).wait_recv()
        start(own_pushes(nb, t))

    def early(n, carry):
        forward(n)
        return carry

    def reached(n):
        mid = jnp.where(n < 12, 3 * (jnp.maximum(n, 0) // 3) + 3, n + 1)
        return jnp.maximum(ahead, jnp.where(inner == 1, mid, n + 1))

    lax.fori_loop(0, ahead, early, 0)
    took(own.at[nb, nb], own_recv.at[2])

    @pl.when(inner == 0)
    def _():
        for h in (b, nb):
            cross(h, 0, own.at[h, nb, per - 1], in_target).start()
    start(beside_push(nb))
    load_weights.wait()

    def receive(n):
        step = decode(n)
        u, handed, across, served = step[2], step[5], step[7], step[8]

        chip = step[0] // 2

        @pl.when(handed == 1)
        def _():
            took(landed.at[pl.ds(2 * chip, 2), u], res_recv.at[chip, u])

        @pl.when(handed > 1)
        def _():
            took(landed.at[0, u], res_recv.at[chip, u])

        for d in range(2):
            panel = step[d]

            @pl.when(step[3] == 3)
            def _():
                finish(1, panel, u, lambda t: landed[panel, u, t].T)

            @pl.when(hands(jnp.where(step[3] == 3, 0, handed), d))
            def _():
                finish(1, panel, u, lambda t: landed[panel, u, t])

                @pl.when(served == 1)
                def _():
                    emit(across, d, 1, u, lambda t: landed[panel, u, t])

                @pl.when(jnp.where(handed == 3, nb, 0) == 1)
                def _():
                    for t in range(per):
                        shared[0, t, u] = landed[panel, u, t].T

    def settle(n, carry):
        receive(n)
        return carry

    def nearby():
        for p in range(2):
            parity = b if p == 0 else nb
            finish_all(p, w, gram(p, lambda h, a: own[h, parity, :, a]), True)
        for u in range(per):
            arrive_beside(u, c_target)
        took(beside, beside_recv.at[0])
        keep(c_target)
        finish_all(1, c_target, gram(1, lambda h, a: beside[h, :, a]))

    def compute(n, carry):
        lax.fori_loop(reached(n - 1), reached(n), early, 0)

        step = decode(n)
        first, second, u, along, _, handed, kept, across, served = step

        @pl.when(along == 3)
        def _():
            by_halves(step)

        def both(i, carry):
            panel = jnp.where(i == 0, first, second)

            @pl.when(jnp.where(along == 3, 0, i) == 1)
            def _():
                arrive_beside(u, panel)

            @pl.when(hands(jnp.where(along == 3, 0, handed), i))
            def _():
                total = cut(gram(1, lambda h, a: cols[h, panel, u, a]))
                for t in range(per):
                    stage[panel, u, t] = total(t)
                hand(panel, u).start()

            @pl.when(kept == 1)
            def _():
                total = keep(panel)

                @pl.when(served == 1)
                def _():
                    for v in range(per):
                        emit(across, i, 0, v, cut(total, v))

                @pl.when(jnp.where(handed == 3, nb + jnp.where(i == y, 0, 1), 1) == 0)
                def _():
                    for v in range(per):
                        for t in range(per):
                            shared[0, t, v] = cut(total, v)(t).T

            @pl.when(kept == 2)
            def _():
                finish(0, panel, u, cut(gram(0, lambda h, a: cols[h, panel, u, a])))

            return carry

        lax.fori_loop(0, 2, both, 0)

        @pl.when(n == ahead - 1)
        def _():
            nearby()

        @pl.when(n == BATCH)
        def _():
            lax.fori_loop(0, BATCH - LAG, settle, 0)

        @pl.when(n >= BATCH)
        def _():
            receive(n - LAG)

        @pl.when(jnp.where(inner == 0, n, -1) == BATCH)
        def _():
            share().start()

        @pl.when(inner == 1)
        def _():
            @pl.when(n == STEPS - 9)
            def _():
                for h in (b, nb):
                    start(near_own(h, 0))

            @pl.when(n == STEPS - 7)
            def _():
                start(near_own(b, 1))

            @pl.when(n == BATCH + 1)
            def _():
                for d in range(2):
                    direct(d, 0, 0, per - 1).start()
                    direct(d, 1, 0, per - 1).start()
                    direct(d, 0, 1, per - 1).start()
                direct(0, nb, 0, 0).start()

                @pl.when(nb == 0)
                def _():
                    direct(0, 0, 1, 0).start()

            @pl.when(n == STEPS - 4)
            def _():
                start(near_own(nb, 1))
                for h in (b, nb):
                    start(pair_own(h))

            @pl.when(n == STEPS - 3)
            def _():
                took(crossed.at[:, 0], crossed_recv.at[0])
                for h in (b, nb):
                    cross(h, 1, crossed.at[h, 0], c_target).start()

            @pl.when(n == STEPS - 2)
            def _():
                took(crossed.at[:, 1], crossed_recv.at[1])

            @pl.when(jnp.logical_or(n == STEPS - 3, n == STEPS - 2))
            def _():
                d = n - (STEPS - 3)
                total = cut(gram(1, lambda h, a: crossed[h, d, a]))
                finish(1, at(outward, y, jnp.where(d == 0, c, 1 - c)), per - 1, total)
                emit(0, d, 1, per - 1, total)
                direct(d, 1, per - 1, per - 1).start()

                @pl.when(jnp.where(d == 0, nb, 0) == 1)
                def _():
                    direct(0, 1, per - 1, 0).start()

            @pl.when(n == STEPS - 2)
            def _():
                relay(0)

            @pl.when(n == STEPS - 1)
            def _():
                relay(1)

        return carry

    def relay(k):
        p = min(k, 1)
        tiles = range(per) if k == 0 else (k - 1,)
        took(passing.at[:, p] if k == 0 else passing.at[:, p, k - 1], passing_recv.at[k])
        for u in tiles:
            for d in range(2):
                onward(d, p, u).start()

    lax.fori_loop(0, count, compute, 0)

    @pl.when(inner == 1)
    def _():
        near_arrive(0)
        for h in (b, nb):
            start(near_relay(h, 0))
        relay(2)
        receive(count - LAG)
        lax.fori_loop(count - LAG + 1, count - 2, settle, 0)
        near_arrive(1)
        for h in (b, nb):
            start(near_relay(h, 1))
        pair_arrive(0)
        for h in (b, nb):
            start(pair_relay(h))

        def adjacent(d, carry):
            cc = jnp.where(d == 0, c, 1 - c)

            @pl.when(d == 1)
            def _():
                took(near.at[:, 1], near_recv.at[2])
                pair_arrive(1)

            finish_all(1, at(z, 1 - y, cc), gram(1, lambda h, a: near[h, d, :, a]))
            finish(1, at(inward, y, cc), per - 1, cut(gram(1, lambda h, a: pair[h, d, a])))
            return carry

        lax.fori_loop(0, 2, adjacent, 0)

        sent(held.at[:, 0, :5], DIRECT)
        sent(passing, VIA)
        sent(passing, ONWARD)
        sent(near, NEAR)
        sent(pair, PAIR)
        sent(crossed.at[:, 0], CROSS)
        sent(cols.at[0, :11], ALONG)
        sent(cols.at[0, :4], OVER)
        sent(cols.at[:, :8], CORE)

    @pl.when(inner == 0)
    def _():
        def accept(k, t, p):
            d = k % 2
            panel = at(inward, jnp.where(k < 2, y, 1 - y), jnp.where(d == 0, c, 1 - c))
            finish(jnp.where(p == 0, b, nb), panel, t, lambda u: got[k, p, u, t])

        def closer(k, carry):
            @pl.when(k == 0)
            def _():
                for t in range(per - 1):
                    accept(k, t, nb)

            for p in range(2):
                accept(k, per - 1, p)
            return carry

        def farther(k, carry):
            accept(k % 2 + 2, per - 1, k // 2)
            return carry

        lax.fori_loop(count - LAG, count - 2, settle, 0)
        took(held.at[:, 0, :5], got_recv.at[0])
        lax.fori_loop(0, 2, closer, 0)
        took(got.at[2:, :, :, per - 1], got_recv.at[1])
        lax.fori_loop(0, 4, farther, 0)
        sent(cols.at[0, :4], ALONG)
        sent(cols.at[0, :7], OVER)
        sent(cols.at[:, :7], CORE)
        took(shared.at[1], got_recv.at[2])
        for t in range(per):
            finish(1, at(z, 1 - y, jnp.where(y == 1, c, 1 - c)), t, lambda u: shared[1, t, u])
        sent(shared.at[0], SHARE)
        sent(crossed.at[:, 0], CROSS)

    sent(own.at[b], SWAP)
    sent(beside, BESIDE)
    lax.fori_loop(count - 2, count, settle, 0)

    @pl.when(inner == 0)
    def _():
        sent(held.at[:, 0, :21], HAND)

    @pl.when(inner == 1)
    def _():
        sent(held.at[:, 0, :20], HAND)


def ring(resid, samples, precision, active):
    panels = lax.axis_size("wide")
    row_tiles, _, per_class, tile, _ = precision.shape
    per = row_tiles // 2
    half = resid.shape[1]
    depth = panels // 4
    scale = 0.5 / (2 * half)
    any_spec = pl.BlockSpec(memory_space=pl.ANY)
    bf16, f32 = resid.dtype, jnp.float32
    dma = pltpu.SemaphoreType.DMA
    updated = pl.pallas_call(
        functools.partial(kernel, depth, scale),
        out_shape=pltpu.VMEM((per, 2, per_class, tile, tile), f32),
        in_specs=[any_spec, any_spec, any_spec, pl.BlockSpec(memory_space=pltpu.SMEM)],
        out_specs=pl.BlockSpec(memory_space=pltpu.VMEM),
        scratch_shapes=[
            pltpu.VMEM((2, 2, per, 2, tile, half), bf16),
            pltpu.VMEM((2, panels, per, 2, tile, half), bf16),
            pltpu.VMEM((2, per, 2, tile, half), bf16),
            pltpu.VMEM((2, 2, per, 2, tile, half), bf16),
            pltpu.VMEM((2, 2, 2, tile, half), bf16),
            pltpu.VMEM((panels, per, per, tile, tile), f32),
            pltpu.VMEM((panels, per, per, tile, tile), f32),
            pltpu.VMEM((2, 2, 2, per, per, tile, tile), f32),
            pltpu.VMEM((4, 2, per, per, tile, tile), f32),
            pltpu.VMEM((2, 2, per, tile, tile), f32),
            pltpu.VMEM((2, per, per, tile, tile), f32),
            pltpu.VMEM((2, 2, 2, tile, half), bf16),
            dma((2, panels // 2, per)),
            dma((panels // 2, per)),
            dma((3,)),
            dma((panels // 2, per)),
            dma((4,)),
            dma((1,)),
            dma((3,)),
            dma((2,)),
            dma((3,)),
            dma((3,)),
            dma((13,)),
            dma((2,)),
            dma((2,)),
        ],
        compiler_params=pltpu.CompilerParams(
            collective_id=0, has_side_effects=True, vmem_limit_bytes=52 * 1024 * 1024
        ),
    )(
        resid.reshape(per, 2, tile, half),
        samples.reshape(per, 2, tile, half),
        precision.reshape(per, 2, per_class, tile, tile),
        active[:, 0],
    )
    return updated.reshape(precision.shape)


def body(resid, samples, precision, active):
    panels = lax.axis_size("wide")
    row_tiles, _, per_class, tile, _ = precision.shape
    words = 8 * per_class * row_tiles * tile * tile + 4 * panels * row_tiles * tile * resid.shape[1]
    if lax.axis_size("blk") == 2 and panels // 4 == 4 and row_tiles == 4 and words < 52 * 1024 * 1024:
        return ring(resid, samples, precision, active)
    return local(resid, samples, precision, active)


def solution(mesh):
    in_specs = (
        P("wide", "blk"),
        P("wide", "blk"),
        P("wide", "blk", None, None, None),
        P("wide", "blk", None),
    )
    out_specs = P("wide", "blk", None, None, None)
    return jax.shard_map(body, mesh=mesh, in_specs=in_specs, out_specs=out_specs, check_vma=False)
```

```python
import functools

import jax
import jax.numpy as jnp
from jax import lax
from jax.experimental import pallas as pl
from jax.experimental.pallas import tpu as pltpu
from jax.sharding import PartitionSpec as P

STEP = 1.0
LASSO = 0.1
RIDGE = 0.5


def local(resid, samples, precision, active):
    groups = lax.axis_size("blk")
    column_group = lax.axis_index("blk")
    panel_index = lax.axis_index("wide")
    row_tiles = precision.shape[0]
    per_class = precision.shape[2]
    tile_size = precision.shape[3]
    tiles = per_class * groups
    local_samples = resid.shape[1]
    total_samples = local_samples * groups
    own_rows = panel_index * row_tiles + jnp.arange(row_tiles, dtype=jnp.int32)
    first_column = (column_group - own_rows) % groups
    own_resid = resid.reshape(row_tiles, tile_size, local_samples)
    own_data = samples.reshape(row_tiles, tile_size, local_samples)
    all_resid, all_data = (
        lax.all_gather(resid, "wide", axis=0, tiled=True),
        lax.all_gather(samples, "wide", axis=0, tiled=True),
    )
    resid_tiles = all_resid.reshape(tiles, tile_size, local_samples)
    data_tiles = all_data.reshape(tiles, tile_size, local_samples)
    positions = jnp.arange(per_class * lax.axis_size("blk"), dtype=jnp.int32)
    classes = positions // per_class
    within = positions % per_class
    column_ids = (classes[:, None] - own_rows[None, :]) % groups + groups * within[:, None]
    forward = jnp.einsum(
        "kis,pkjs->pkij", own_resid, data_tiles[column_ids], preferred_element_type=jnp.float32
    )
    backward = jnp.einsum(
        "kis,pkjs->pkij", own_data, resid_tiles[column_ids], preferred_element_type=jnp.float32
    )
    summed = (
        lax.psum_scatter(0.5 * (forward + backward), "blk", scatter_dimension=0, tiled=True)
        / total_samples
    )
    precision_tiles = precision[:, 0]
    active_flags = active[:, 0].astype(jnp.float32)
    gradient_part = summed.transpose(1, 0, 2, 3)
    column_ids = first_column[:, None] + groups * jnp.arange(per_class, dtype=jnp.int32)[None, :]
    same_tile = column_ids == own_rows[:, None]
    identity = jnp.eye(tile_size, dtype=bool)
    on_diag = same_tile[:, :, None, None] & identity
    inverse = jnp.where(on_diag, 1.0 / jnp.where(on_diag, precision_tiles, 1.0), 0.0)
    stepped = precision_tiles - STEP * (gradient_part + RIDGE * precision_tiles - inverse)
    shrunk = jnp.sign(stepped) * jnp.maximum(jnp.abs(stepped) - STEP * LASSO, 0.0)
    updated = jnp.where(on_diag, stepped, shrunk) * active_flags[:, :, None, None]
    return updated[:, None]


MESH = pl.DeviceIdType.MESH

END = (
    (0, 1, 0, 1, 0, 3, 0), (1, 0, 0, 0, 1, 2, 2), (0, 1, 1, 1, 0, 4, 1), (2, 0, 0, 0, 1, 1, 0),
    (1, 1, 0, 0, 0, 1, 2), (2, 0, 1, 0, 1, 1, 1), (2, 1, 0, 0, 0, 1, 0), (3, 0, 0, 0, 1, 1, 0),
    (2, 1, 1, 0, 0, 1, 1), (3, 0, 1, 0, 2, 1, 1), (3, 1, 0, 0, 0, 1, 0), (3, 1, 1, 3, 0, 1, 1),
)
INNER = (
    (2, 0, 0, 2, 1, 1, 0), (0, 0, 0, 1, 0, 1, 0), (1, 1, 0, 0, 0, 0, 0), (2, 0, 1, 2, 1, 0, 1),
    (0, 0, 1, 1, 0, 0, 1), (1, 1, 1, 0, 0, 0, 1), (3, 0, 0, 2, 0, 1, 0), (0, 1, 0, 1, 0, 1, 0),
    (2, 1, 0, 0, 0, 1, 0), (3, 0, 1, 2, 0, 1, 1), (0, 1, 1, 1, 0, 1, 1), (2, 1, 1, 0, 0, 1, 1),
    (3, 1, 0, 0, 0, 1, 0), (3, 1, 1, 0, 0, 1, 1),
)
STEPS = len(INNER)
EARLY = (3, 6)
LAG = 3
BATCH = 8
PARTS = 4
ALONG, OVER, CORE, HAND, SWAP, BESIDE, NEAR, PAIR, DIRECT, VIA, ONWARD, SHARE, CROSS = range(13)


def packed(row):
    place, across, u, along, over, handed, kept = row
    return place + 4 * across + 8 * u + 16 * along + 64 * over + 256 * handed + 2048 * kept


def kernel(
    depth, scale, resid, samples, weights, flags, held,
    own, cols, beside, near, pair, stage, landed, out, got, passing, shared, crossed, recv, beside_cols, own_recv,
    res_recv, halves, beside_recv, near_recv, pair_recv, got_recv, passing_recv, sends, crossed_recv, fill,
):
    b = lax.axis_index("blk")
    w = lax.axis_index("wide")
    nb = 1 - b
    z, y, c = w // 4, (w // 2) % 2, w % 2
    per = own.shape[2]
    tile = own.shape[4]
    last = depth - 1
    half = z // 2
    inner = jnp.where(z == 0, 0, jnp.where(z == last, 0, 1))
    inward = z + 1 - 2 * half
    outward = jnp.where(inner == 1, z - 1 + 2 * half, inward)

    def at(zz, yy, cc):
        return (zz * 2 + yy) * 2 + cc

    in_target, out_target = at(inward, y, c), at(outward, y, c)
    y_target, c_target = at(z, 1 - y, c), at(z, y, 1 - c)
    count = len(END) + (len(INNER) - len(END)) * inner
    ahead = EARLY[0] + (EARLY[1] - EARLY[0]) * inner

    def decode(n):
        end, mid = jnp.int32(packed(END[0])), jnp.int32(packed(INNER[0]))
        for k in range(1, STEPS):
            if k < len(END):
                end = jnp.where(n == k, jnp.int32(packed(END[k])), end)
            mid = jnp.where(n == k, jnp.int32(packed(INNER[k])), mid)
        code = jnp.where(inner == 1, mid, end)
        place = code % 4
        zz = jnp.where(half == 0, place, last - place)
        across = (code // 4) % 2
        yy = jnp.where(across == 1, 1 - y, y)
        u = (code // 8) % 2
        along = (code // 16) % 4
        over = (code // 64) % 4
        handed = (code // 256) % 8
        kept = code // 2048
        served = jnp.where(place == 0, 1 + inner, 0)
        return at(zz, yy, c), at(zz, yy, 1 - c), u, along, over, handed, kept, across, served

    loads = []
    for a, src in enumerate((resid, samples)):
        for p in range(2):
            loads.append(
                pltpu.make_async_copy(src.at[:, p], own.at[b, p, :, a], fill.at[0])
            )
    for load in loads:
        load.start()
    load_weights = pltpu.make_async_copy(weights, held, fill.at[1])

    barrier = pltpu.get_barrier_semaphore()

    def greet(**device):
        pl.semaphore_signal(barrier, inc=1, device_id=device, device_id_type=MESH)

    greet(blk=nb)
    greet(wide=y_target)
    greet(wide=c_target)
    greet(wide=in_target)

    @pl.when(inner == 1)
    def _():
        greet(wide=out_target)

    greet(wide=at(outward, y, 1 - c))
    greet(wide=at(z, 1 - y, 1 - c))
    pl.semaphore_wait(barrier, 6 + inner)

    def whole(ref, sent_sem, took_sem):
        return pltpu.make_async_remote_copy(
            src_ref=ref, dst_ref=ref, send_sem=sent_sem, recv_sem=took_sem,
            device_id={"wide": y_target}, device_id_type=MESH,
        )

    def took(ref, sem):
        whole(ref, sends.at[0], sem).wait_recv()

    def sent(ref, k):
        whole(ref, sends.at[k], recv.at[0, 0, 0]).wait_send()

    def push(h, u, src, panel, lane, target):
        sem = beside_cols.at[panel // 2, u] if lane == CORE else recv.at[h, panel // 2, u]
        return pltpu.make_async_remote_copy(
            src_ref=src, dst_ref=cols.at[h, panel, u], send_sem=sends.at[lane],
            recv_sem=sem, device_id={"wide": target}, device_id_type=MESH,
        )

    def arrive(h, u, panel):
        took(cols.at[h, panel, u], recv.at[h, panel // 2, u])

    def arrive_beside(u, panel):
        took(cols.at[:, panel, u], beside_cols.at[panel // 2, u])

    def own_pushes(h, u):
        src = own.at[h, b, u]
        return (
            (None, push(h, u, src, w, OVER, y_target)),
            (None, push(h, u, src, w, ALONG, in_target)),
            (None, push(h, u, src, w, CORE, c_target)),
        ) + (((inner == 1, push(h, u, src, w, ALONG, out_target)),) if u == 0 else ())

    def step_pushes(h, step):
        panel, _, u, along, over = step[:5]
        src = cols.at[h, panel, u]
        target = jnp.where(along == 1, in_target, out_target)
        return (
            (along % 3 > 0, push(h, u, src, panel, ALONG, target)),
            (over == 1, push(h, u, src, panel, OVER, y_target)),
            (None, push(h, u, src, panel, CORE, c_target)),
        )

    def beside_push(h):
        return ((None, pltpu.make_async_remote_copy(
            src_ref=own.at[h, nb], dst_ref=beside.at[h], send_sem=sends.at[BESIDE],
            recv_sem=beside_recv.at[0], device_id={"wide": c_target}, device_id_type=MESH,
        )),)

    def near_push(h, d, u, src, target):
        return ((None, pltpu.make_async_remote_copy(
            src_ref=src, dst_ref=near.at[h, d, u], send_sem=sends.at[NEAR],
            recv_sem=near_recv.at[u if d == 0 else 2], device_id={"wide": target}, device_id_type=MESH,
        )),)

    def near_own(h, u):
        return near_push(h, 0, u, own.at[h, nb, u], y_target)

    def near_relay(h, u):
        return near_push(h, 1, u, near.at[h, 0, u], c_target)

    def near_arrive(u):
        took(near.at[:, 0, u], near_recv.at[u])

    def pair_push(h, d, src, target):
        return ((None, pltpu.make_async_remote_copy(
            src_ref=src, dst_ref=pair.at[h, d], send_sem=sends.at[PAIR],
            recv_sem=pair_recv.at[d], device_id={"wide": target}, device_id_type=MESH,
        )),)

    def pair_own(h):
        return pair_push(h, 0, own.at[h, nb, per - 1], in_target)

    def pair_relay(h):
        return pair_push(h, 1, pair.at[h, 0], c_target)

    def pair_arrive(d):
        took(pair.at[:, d], pair_recv.at[d])

    def share():
        return pltpu.make_async_remote_copy(
            src_ref=shared.at[0], dst_ref=shared.at[1], send_sem=sends.at[SHARE],
            recv_sem=got_recv.at[2], device_id={"wide": at(z, 1 - y, jnp.where(y == 0, c, 1 - c))},
            device_id_type=MESH,
        )

    def hands(handed, d):
        alone = jnp.where(handed == 2, 1, jnp.where(handed >= 3, y, -1))
        return jnp.logical_or(handed == 1, alone == d)

    def lower(handed, d):
        return jnp.where(handed == 4, jnp.where(d == y, 0, 1), 0) == 1

    def cross(h, d, src, target):
        return pltpu.make_async_remote_copy(
            src_ref=src, dst_ref=crossed.at[h, d], send_sem=sends.at[CROSS],
            recv_sem=crossed_recv.at[d], device_id={"wide": target}, device_id_type=MESH,
        )

    def outward_core(d):
        return at(outward, y, jnp.where(d == 0, c, 1 - c))

    def direct(d, p, u, t):
        return pltpu.make_async_remote_copy(
            src_ref=out.at[0, d, p, u, t], dst_ref=got.at[d, p, u, t],
            send_sem=sends.at[DIRECT], recv_sem=got_recv.at[0],
            device_id={"wide": outward_core(d)}, device_id_type=MESH,
        )

    def via(d, p, u):
        return pltpu.make_async_remote_copy(
            src_ref=out.at[1, d, p, u, per - 1], dst_ref=passing.at[d, p, u],
            send_sem=sends.at[VIA], recv_sem=passing_recv.at[p * (1 + u)],
            device_id={"wide": y_target}, device_id_type=MESH,
        )

    def onward(d, p, u):
        return pltpu.make_async_remote_copy(
            src_ref=passing.at[d, p, u], dst_ref=got.at[2 + d, p, u, per - 1],
            send_sem=sends.at[ONWARD], recv_sem=got_recv.at[1],
            device_id={"wide": outward_core(d)}, device_id_type=MESH,
        )

    def start(pushes):
        for when, copy in pushes:
            if when is None:
                copy.start()
            else:
                pl.when(when)(copy.start)

    def swap(h, i, t):
        p = (nb, b)[i] if h is b else (b, nb)[i]
        return pltpu.make_async_remote_copy(
            src_ref=own.at[h, p, t], dst_ref=own.at[h, p, t], send_sem=sends.at[SWAP],
            recv_sem=own_recv.at[2 * i + t], device_id={"blk": nb}, device_id_type=MESH,
        )

    def hand(panel, u):
        return pltpu.make_async_remote_copy(
            src_ref=stage.at[panel, u], dst_ref=landed.at[panel, u],
            send_sem=sends.at[HAND], recv_sem=res_recv.at[panel // 2, u],
            device_id={"blk": nb}, device_id_type=MESH,
        )

    def gram(p, side):
        total = None
        for h in range(2):
            for a in range(2):
                left = own[h, p, :, a].reshape(per * tile, -1)
                right = side(h, 1 - a).reshape(-1, own.shape[5])
                part = lax.dot_general(
                    left, right, (((1,), (1,)), ((), ())), preferred_element_type=jnp.float32
                )
                total = part if total is None else total + part
        return total * scale

    def finish(p, panel, u, part, diagonal=False, rows=None):
        for t in range(per) if rows is None else rows:
            slot = panel * per + u
            weight = held[t, p, slot]
            half = part(t) + RIDGE * weight
            if diagonal and t == u:
                lines = lax.broadcasted_iota(jnp.int32, (tile, tile), 0)
                columns = lax.broadcasted_iota(jnp.int32, (tile, tile), 1)
                on_diag = lines == columns + b * (2 * tile)
                inverse = jnp.where(on_diag, 1.0 / jnp.where(on_diag, weight, 1.0), 0.0)
                stepped = weight - STEP * (half - inverse)
            else:
                stepped = weight - STEP * half
            bound = STEP * LASSO
            updated = stepped - jnp.clip(stepped, -bound, bound)
            if diagonal and t == u:
                updated = jnp.where(on_diag, stepped, updated)
            flag = flags[2 * t + p, slot].astype(jnp.float32)
            held[t, p, slot] = updated * flag

    def cut(total, u=0):
        return lambda t: total[t * tile:(t + 1) * tile, u * tile:(u + 1) * tile]

    def finish_all(p, panel, total, diagonal=False):
        for u in range(per):
            finish(p, panel, u, cut(total, u), diagonal)

    def keep(panel):
        total = gram(0, lambda h, a: cols[h, panel, :, a])
        finish_all(0, panel, total)
        return total

    def emit(across, d, p, u, part):
        t = per - 1
        out[across, d, p, u, t] = part(t).T

        @pl.when(across == 1)
        def _():
            via(d, p, u).start()

        @pl.when(jnp.where(across + d == 0, nb, -1) == p)
        def _():
            for t in range(per - 1):
                out[0, d, p, u, t] = part(t).T

    def pass_on(h, step):
        arrive(h, step[2], step[0])
        start(step_pushes(h, step))

    def piece(ref, h, panel, u, j):
        return ref.at[h, panel, u, :, pl.ds(j * (tile // PARTS), tile // PARTS)]

    def half_push(h, panel, u, j, lane, target):
        sem = halves.at[PARTS + j] if lane == CORE else halves.at[j]
        return pltpu.make_async_remote_copy(
            src_ref=piece(cols, h, panel, u, j), dst_ref=piece(cols, h, panel, u, j),
            send_sem=sends.at[lane], recv_sem=sem, device_id={"wide": target},
            device_id_type=MESH,
        )

    def half_hand(panel, u, j):
        rows = pl.ds(j * (tile // PARTS), tile // PARTS)
        return pltpu.make_async_remote_copy(
            src_ref=stage.at[panel, u, :, rows], dst_ref=landed.at[panel, u, :, rows],
            send_sem=sends.at[HAND], recv_sem=res_recv.at[panel // 2, u],
            device_id={"blk": nb}, device_id_type=MESH,
        )

    def by_halves(step):
        u = step[2]
        for j in range(PARTS):
            rows = pl.ds(j * (tile // PARTS), tile // PARTS)
            for d in range(2):
                panel = step[d]
                took(cols.at[:, panel, u, :, rows], halves.at[PARTS * d + j])
                if d == 0:
                    for h in (b, nb):
                        half_push(h, panel, u, j, CORE, c_target).start()
                total = None
                for h in range(2):
                    for a in range(2):
                        part = lax.dot_general(
                            cols[h, panel, u, a, rows],
                            own[h, 1, :, 1 - a].reshape(per * tile, -1),
                            (((1,), (1,)), ((), ())), preferred_element_type=jnp.float32,
                        )
                        total = part if total is None else total + part
                total = total * scale
                for t in range(per):
                    stage[panel, u, t, rows] = total[:, t * tile:(t + 1) * tile]
                half_hand(panel, u, j).start()

    def forward(n):
        step = decode(n)

        @pl.when(step[3] < 3)
        def _():
            for h in (b, nb):
                pass_on(h, step)

        @pl.when(step[4] == 2)
        def _():
            for j in range(PARTS):
                for h in (b, nb):
                    half_push(h, step[0], step[2], j, OVER, y_target).start()

    pltpu.make_async_copy(own.at[b], own.at[b], fill.at[0]).wait()
    for i in range(2):
        for t in range(per):
            swap(b, i, t).start()
    for t in range(per):
        start(own_pushes(b, t))
    load_weights.start()
    start(beside_push(b))
    for t in range(per):
        swap(nb, 0, t).wait_recv()
        start(own_pushes(nb, t))

    def early(n, carry):
        forward(n)
        return carry

    def reached(n):
        mid = jnp.where(n < 12, 3 * (jnp.maximum(n, 0) // 3) + 3, n + 1)
        return jnp.maximum(ahead, jnp.where(inner == 1, mid, n + 1))

    def row_hand(panel, u, t, lane=HAND):
        total = None
        for h in range(2):
            for a in range(2):
                part = lax.dot_general(
                    own[h, 1, t, a], cols[h, panel, u, 1 - a], (((1,), (1,)), ((), ())),
                    preferred_element_type=jnp.float32,
                )
                total = part if total is None else total + part
        stage[panel, u, t] = total * scale
        pltpu.make_async_remote_copy(
            src_ref=stage.at[panel, u, t], dst_ref=landed.at[panel, u, t],
            send_sem=sends.at[lane], recv_sem=res_recv.at[panel // 2, u],
            device_id={"blk": nb}, device_id_type=MESH,
        ).start()

    lax.fori_loop(0, 2, early, 0)
    took(own.at[nb, nb, 0], own_recv.at[2])

    @pl.when(inner == 0)
    def _():
        def first_row(n, carry):
            first, second, u = decode(n)[:3]
            arrive_beside(u, second)
            row_hand(jnp.where(jnp.where(n == 0, y, 1) == 0, first, second), u, 0)
            return carry

        lax.fori_loop(0, 2, first_row, 0)

    lax.fori_loop(2, ahead, early, 0)
    for t in range(1, per):
        took(own.at[nb, nb, t], own_recv.at[2 + t])

    @pl.when(inner == 0)
    def _():
        for h in (b, nb):
            cross(h, 0, own.at[h, nb, per - 1], in_target).start()
    start(beside_push(nb))
    load_weights.wait()

    def receive(n):
        step = decode(n)
        u, handed, across, served = step[2], step[5], step[7], step[8]

        chip = step[0] // 2

        @pl.when(handed == 1)
        def _():
            took(landed.at[pl.ds(2 * chip, 2), u], res_recv.at[chip, u])

        @pl.when(jnp.where(handed == 4, 0, handed) > 1)
        def _():
            took(landed.at[0, u], res_recv.at[chip, u])

        @pl.when(handed == 4)
        def _():
            took(held.at[0, 0, :3], res_recv.at[chip, u])

        for d in range(2):
            panel = step[d]

            @pl.when(lower(handed, d))
            def _():
                finish(1, panel, u, lambda t: landed[panel, u, t], rows=(per - 1,))

            @pl.when(step[3] == 3)
            def _():
                finish(1, panel, u, lambda t: landed[panel, u, t].T)

            @pl.when(hands(jnp.where(step[3] == 3, 0, handed), d))
            def _():
                finish(1, panel, u, lambda t: landed[panel, u, t])

                @pl.when(served == 2)
                def _():
                    emit(across, d, 1, u, lambda t: landed[panel, u, t])

                @pl.when(jnp.where(served == 1, nb + jnp.where(d == y, 1, 0), 0) == 2)
                def _():
                    shared[0, u] = landed[panel, u, 0].T

                    @pl.when(u == 0)
                    def _():
                        shared[0, 2] = landed[panel, u, 1].T

    def settle(n, carry):
        receive(n)
        return carry

    def nearby():
        for p in range(2):
            parity = b if p == 0 else nb
            finish_all(p, w, gram(p, lambda h, a: own[h, parity, :, a]), True)
        for u in range(per):
            arrive_beside(u, c_target)
        took(beside, beside_recv.at[0])
        keep(c_target)
        finish_all(1, c_target, gram(1, lambda h, a: beside[h, :, a]))

    def compute(n, carry):
        lax.fori_loop(reached(n - 1), reached(n), early, 0)

        step = decode(n)
        first, second, u, along, _, handed, kept, across, served = step

        begun = jnp.logical_and(n < 2, inner == 0)

        @pl.when(along == 3)
        def _():
            by_halves(step)

        def both(i, carry):
            panel = jnp.where(i == 0, first, second)

            @pl.when(jnp.where(along == 3, 0, jnp.where(begun, 0, i)) == 1)
            def _():
                arrive_beside(u, panel)

            @pl.when(hands(jnp.where(begun, handed, 0), i))
            def _():
                for t in range(1, per):
                    row_hand(panel, u, t)

            @pl.when(hands(jnp.where(along == 3, 0, jnp.where(begun, 0, handed)), i))
            def _():
                total = cut(gram(1, lambda h, a: cols[h, panel, u, a]))
                for t in range(per):
                    stage[panel, u, t] = total(t)
                hand(panel, u).start()

            @pl.when(lower(handed, i))
            def _():
                row_hand(panel, u, per - 1, SHARE)

            @pl.when(kept == 1)
            def _():
                total = keep(panel)

                @pl.when(served == 2)
                def _():
                    for v in range(per):
                        emit(across, i, 0, v, cut(total, v))

                @pl.when(jnp.where(served == 1, nb + jnp.where(i == y, 0, 1), 1) == 0)
                def _():
                    for v in range(per):
                        shared[0, v] = cut(total, v)(0).T
                    shared[0, 2] = cut(total, 0)(1).T

            @pl.when(kept == 2)
            def _():
                finish(0, panel, u, cut(gram(0, lambda h, a: cols[h, panel, u, a])))

            return carry

        lax.fori_loop(0, 2, both, 0)

        @pl.when(n == ahead - 1)
        def _():
            nearby()

        @pl.when(n == BATCH)
        def _():
            lax.fori_loop(0, BATCH - LAG, settle, 0)

        @pl.when(n >= BATCH)
        def _():
            receive(n - LAG)

        @pl.when(jnp.where(inner == 0, n, -1) == BATCH + 1)
        def _():
            share().start()

        @pl.when(inner == 1)
        def _():
            @pl.when(n == STEPS - 9)
            def _():
                for h in (b, nb):
                    start(near_own(h, 0))

            @pl.when(n == STEPS - 7)
            def _():
                start(near_own(b, 1))

            @pl.when(n == BATCH + 1)
            def _():
                for d in range(2):
                    direct(d, 0, 0, per - 1).start()
                    direct(d, 1, 0, per - 1).start()
                    direct(d, 0, 1, per - 1).start()
                direct(0, nb, 0, 0).start()

                @pl.when(nb == 0)
                def _():
                    direct(0, 0, 1, 0).start()

            @pl.when(n == STEPS - 4)
            def _():
                start(near_own(nb, 1))
                for h in (b, nb):
                    start(pair_own(h))

            @pl.when(n == STEPS - 3)
            def _():
                took(crossed.at[:, 0], crossed_recv.at[0])
                for h in (b, nb):
                    cross(h, 1, crossed.at[h, 0], c_target).start()

            @pl.when(n == STEPS - 2)
            def _():
                took(crossed.at[:, 1], crossed_recv.at[1])

            @pl.when(jnp.logical_or(n == STEPS - 3, n == STEPS - 2))
            def _():
                d = n - (STEPS - 3)
                total = cut(gram(1, lambda h, a: crossed[h, d, a]))
                finish(1, at(outward, y, jnp.where(d == 0, c, 1 - c)), per - 1, total)
                emit(0, d, 1, per - 1, total)
                direct(d, 1, per - 1, per - 1).start()

                @pl.when(jnp.where(d == 0, nb, 0) == 1)
                def _():
                    direct(0, 1, per - 1, 0).start()

            @pl.when(n == STEPS - 2)
            def _():
                relay(0)

            @pl.when(n == STEPS - 1)
            def _():
                relay(1)

        return carry

    def relay(k):
        p = min(k, 1)
        tiles = range(per) if k == 0 else (k - 1,)
        took(passing.at[:, p] if k == 0 else passing.at[:, p, k - 1], passing_recv.at[k])
        for u in tiles:
            for d in range(2):
                onward(d, p, u).start()

    lax.fori_loop(0, count, compute, 0)

    @pl.when(inner == 1)
    def _():
        near_arrive(0)
        for h in (b, nb):
            start(near_relay(h, 0))
        relay(2)
        receive(count - LAG)
        lax.fori_loop(count - LAG + 1, count - 2, settle, 0)
        near_arrive(1)
        for h in (b, nb):
            start(near_relay(h, 1))
        pair_arrive(0)
        for h in (b, nb):
            start(pair_relay(h))

        def adjacent(d, carry):
            cc = jnp.where(d == 0, c, 1 - c)

            @pl.when(d == 1)
            def _():
                took(near.at[:, 1], near_recv.at[2])
                pair_arrive(1)

            finish_all(1, at(z, 1 - y, cc), gram(1, lambda h, a: near[h, d, :, a]))
            finish(1, at(inward, y, cc), per - 1, cut(gram(1, lambda h, a: pair[h, d, a])))
            return carry

        lax.fori_loop(0, 2, adjacent, 0)

        sent(held.at[:, 0, :5], DIRECT)
        sent(passing, VIA)
        sent(passing, ONWARD)
        sent(near, NEAR)
        sent(pair, PAIR)
        sent(crossed.at[:, 0], CROSS)
        sent(cols.at[0, :11], ALONG)
        sent(cols.at[0, :4], OVER)
        sent(cols.at[:, :8], CORE)

    @pl.when(inner == 0)
    def _():
        def accept(k, t, p):
            d = k % 2
            panel = at(inward, jnp.where(k < 2, y, 1 - y), jnp.where(d == 0, c, 1 - c))
            finish(jnp.where(p == 0, b, nb), panel, t, lambda u: got[k, p, u, t])

        def closer(k, carry):
            @pl.when(k == 0)
            def _():
                for t in range(per - 1):
                    accept(k, t, nb)

            for p in range(2):
                accept(k, per - 1, p)
            return carry

        def farther(k, carry):
            accept(k % 2 + 2, per - 1, k // 2)
            return carry

        lax.fori_loop(count - LAG, count - 2, settle, 0)
        took(held.at[:, 0, :5], got_recv.at[0])
        lax.fori_loop(0, 2, closer, 0)
        took(got.at[2:, :, :, per - 1], got_recv.at[1])
        lax.fori_loop(0, 4, farther, 0)
        sent(cols.at[0, :4], ALONG)
        sent(cols.at[0, :7], OVER)
        sent(cols.at[:, :7], CORE)
        took(shared.at[1], got_recv.at[2])
        other = at(z, 1 - y, jnp.where(y == 1, c, 1 - c))
        finish(1, other, 0, lambda t: shared[1, t])
        finish(1, other, 1, lambda t: shared[1, 2], rows=(0,))
        sent(held.at[0, 0, :4], SHARE)
        sent(crossed.at[:, 0], CROSS)

    sent(own.at[b], SWAP)
    sent(beside, BESIDE)
    lax.fori_loop(count - 2, count, settle, 0)

    @pl.when(inner == 0)
    def _():
        sent(held.at[:, 0, :21], HAND)

    @pl.when(inner == 1)
    def _():
        sent(held.at[:, 0, :20], HAND)


def ring(resid, samples, precision, active):
    panels = lax.axis_size("wide")
    row_tiles, _, per_class, tile, _ = precision.shape
    per = row_tiles // 2
    half = resid.shape[1]
    depth = panels // 4
    scale = 0.5 / (2 * half)
    any_spec = pl.BlockSpec(memory_space=pl.ANY)
    bf16, f32 = resid.dtype, jnp.float32
    dma = pltpu.SemaphoreType.DMA
    updated = pl.pallas_call(
        functools.partial(kernel, depth, scale),
        out_shape=pltpu.VMEM((per, 2, per_class, tile, tile), f32),
        in_specs=[any_spec, any_spec, any_spec, pl.BlockSpec(memory_space=pltpu.SMEM)],
        out_specs=pl.BlockSpec(memory_space=pltpu.VMEM),
        scratch_shapes=[
            pltpu.VMEM((2, 2, per, 2, tile, half), bf16),
            pltpu.VMEM((2, panels, per, 2, tile, half), bf16),
            pltpu.VMEM((2, per, 2, tile, half), bf16),
            pltpu.VMEM((2, 2, per, 2, tile, half), bf16),
            pltpu.VMEM((2, 2, 2, tile, half), bf16),
            pltpu.VMEM((panels, per, per, tile, tile), f32),
            pltpu.VMEM((panels, per, per, tile, tile), f32),
            pltpu.VMEM((2, 2, 2, per, per, tile, tile), f32),
            pltpu.VMEM((4, 2, per, per, tile, tile), f32),
            pltpu.VMEM((2, 2, per, tile, tile), f32),
            pltpu.VMEM((2, per + 1, tile, tile), f32),
            pltpu.VMEM((2, 2, 2, tile, half), bf16),
            dma((2, panels // 2, per)),
            dma((panels // 2, per)),
            dma((4,)),
            dma((panels // 2, per)),
            dma((2 * PARTS,)),
            dma((1,)),
            dma((3,)),
            dma((2,)),
            dma((3,)),
            dma((3,)),
            dma((13,)),
            dma((2,)),
            dma((2,)),
        ],
        compiler_params=pltpu.CompilerParams(
            collective_id=0, has_side_effects=True, vmem_limit_bytes=52 * 1024 * 1024
        ),
    )(
        resid.reshape(per, 2, tile, half),
        samples.reshape(per, 2, tile, half),
        precision.reshape(per, 2, per_class, tile, tile),
        active[:, 0],
    )
    return updated.reshape(precision.shape)


def body(resid, samples, precision, active):
    panels = lax.axis_size("wide")
    row_tiles, _, per_class, tile, _ = precision.shape
    words = 8 * per_class * row_tiles * tile * tile + 4 * panels * row_tiles * tile * resid.shape[1]
    if lax.axis_size("blk") == 2 and panels // 4 == 4 and row_tiles == 4 and words < 52 * 1024 * 1024:
        return ring(resid, samples, precision, active)
    return local(resid, samples, precision, active)


def solution(mesh):
    in_specs = (
        P("wide", "blk"),
        P("wide", "blk"),
        P("wide", "blk", None, None, None),
        P("wide", "blk", None),
    )
    out_specs = P("wide", "blk", None, None, None)
    return jax.shard_map(body, mesh=mesh, in_specs=in_specs, out_specs=out_specs, check_vma=False)
```

```python
import functools

import jax
import jax.numpy as jnp
from jax import lax
from jax.experimental import pallas as pl
from jax.experimental.pallas import tpu as pltpu
from jax.sharding import PartitionSpec as P

STEP = 1.0
LASSO = 0.1
RIDGE = 0.5


def local(resid, samples, precision, active):
    groups = lax.axis_size("blk")
    column_group = lax.axis_index("blk")
    panel_index = lax.axis_index("wide")
    row_tiles = precision.shape[0]
    per_class = precision.shape[2]
    tile_size = precision.shape[3]
    tiles = per_class * groups
    local_samples = resid.shape[1]
    total_samples = local_samples * groups
    own_rows = panel_index * row_tiles + jnp.arange(row_tiles, dtype=jnp.int32)
    first_column = (column_group - own_rows) % groups
    own_resid = resid.reshape(row_tiles, tile_size, local_samples)
    own_data = samples.reshape(row_tiles, tile_size, local_samples)
    all_resid, all_data = (
        lax.all_gather(resid, "wide", axis=0, tiled=True),
        lax.all_gather(samples, "wide", axis=0, tiled=True),
    )
    resid_tiles = all_resid.reshape(tiles, tile_size, local_samples)
    data_tiles = all_data.reshape(tiles, tile_size, local_samples)
    positions = jnp.arange(per_class * lax.axis_size("blk"), dtype=jnp.int32)
    classes = positions // per_class
    within = positions % per_class
    column_ids = (classes[:, None] - own_rows[None, :]) % groups + groups * within[:, None]
    forward = jnp.einsum(
        "kis,pkjs->pkij", own_resid, data_tiles[column_ids], preferred_element_type=jnp.float32
    )
    backward = jnp.einsum(
        "kis,pkjs->pkij", own_data, resid_tiles[column_ids], preferred_element_type=jnp.float32
    )
    summed = (
        lax.psum_scatter(0.5 * (forward + backward), "blk", scatter_dimension=0, tiled=True)
        / total_samples
    )
    precision_tiles = precision[:, 0]
    active_flags = active[:, 0].astype(jnp.float32)
    gradient_part = summed.transpose(1, 0, 2, 3)
    column_ids = first_column[:, None] + groups * jnp.arange(per_class, dtype=jnp.int32)[None, :]
    same_tile = column_ids == own_rows[:, None]
    identity = jnp.eye(tile_size, dtype=bool)
    on_diag = same_tile[:, :, None, None] & identity
    inverse = jnp.where(on_diag, 1.0 / jnp.where(on_diag, precision_tiles, 1.0), 0.0)
    stepped = precision_tiles - STEP * (gradient_part + RIDGE * precision_tiles - inverse)
    shrunk = jnp.sign(stepped) * jnp.maximum(jnp.abs(stepped) - STEP * LASSO, 0.0)
    updated = jnp.where(on_diag, stepped, shrunk) * active_flags[:, :, None, None]
    return updated[:, None]


MESH = pl.DeviceIdType.MESH

END = (
    (0, 1, 0, 1, 0, 3, 0), (1, 0, 0, 0, 1, 2, 2), (0, 1, 1, 1, 0, 3, 1), (2, 0, 0, 0, 1, 1, 0),
    (1, 1, 0, 0, 0, 1, 2), (2, 0, 1, 0, 1, 1, 1), (2, 1, 0, 0, 0, 1, 0), (3, 0, 0, 0, 1, 1, 0),
    (2, 1, 1, 0, 0, 1, 1), (3, 0, 1, 0, 2, 1, 1), (3, 1, 0, 0, 0, 1, 0), (3, 1, 1, 3, 0, 1, 1),
)
INNER = (
    (2, 0, 0, 2, 1, 1, 0), (0, 0, 0, 1, 0, 1, 0), (1, 1, 0, 0, 0, 0, 0), (2, 0, 1, 2, 1, 0, 1),
    (0, 0, 1, 1, 0, 0, 1), (1, 1, 1, 0, 0, 0, 1), (3, 0, 0, 2, 0, 1, 0), (0, 1, 0, 1, 0, 1, 0),
    (2, 1, 0, 0, 0, 1, 0), (3, 0, 1, 2, 0, 1, 1), (0, 1, 1, 1, 0, 1, 1), (2, 1, 1, 0, 0, 1, 1),
    (3, 1, 0, 0, 0, 1, 0), (3, 1, 1, 0, 0, 1, 1),
)
STEPS = len(INNER)
EARLY = (3, 6)
LAG = 3
BATCH = 8
PARTS = 4
ALONG, OVER, CORE, HAND, SWAP, BESIDE, NEAR, PAIR, DIRECT, VIA, ONWARD, SHARE, CROSS = range(13)


def packed(row):
    place, across, u, along, over, handed, kept = row
    return place + 4 * across + 8 * u + 16 * along + 64 * over + 256 * handed + 2048 * kept


def kernel(
    depth, scale, resid, samples, weights, flags, held,
    own, cols, beside, near, pair, stage, landed, out, got, passing, shared, crossed, recv, beside_cols, own_recv,
    res_recv, halves, beside_recv, near_recv, pair_recv, got_recv, passing_recv, sends, crossed_recv, fill,
):
    b = lax.axis_index("blk")
    w = lax.axis_index("wide")
    nb = 1 - b
    z, y, c = w // 4, (w // 2) % 2, w % 2
    per = own.shape[2]
    tile = own.shape[4]
    last = depth - 1
    half = z // 2
    inner = jnp.where(z == 0, 0, jnp.where(z == last, 0, 1))
    inward = z + 1 - 2 * half
    outward = jnp.where(inner == 1, z - 1 + 2 * half, inward)

    def at(zz, yy, cc):
        return (zz * 2 + yy) * 2 + cc

    in_target, out_target = at(inward, y, c), at(outward, y, c)
    y_target, c_target = at(z, 1 - y, c), at(z, y, 1 - c)
    count = len(END) + (len(INNER) - len(END)) * inner
    ahead = EARLY[0] + (EARLY[1] - EARLY[0]) * inner

    def decode(n):
        end, mid = jnp.int32(packed(END[0])), jnp.int32(packed(INNER[0]))
        for k in range(1, STEPS):
            if k < len(END):
                end = jnp.where(n == k, jnp.int32(packed(END[k])), end)
            mid = jnp.where(n == k, jnp.int32(packed(INNER[k])), mid)
        code = jnp.where(inner == 1, mid, end)
        place = code % 4
        zz = jnp.where(half == 0, place, last - place)
        across = (code // 4) % 2
        yy = jnp.where(across == 1, 1 - y, y)
        u = (code // 8) % 2
        along = (code // 16) % 4
        over = (code // 64) % 4
        handed = (code // 256) % 8
        kept = code // 2048
        served = jnp.where(place == 0, 1 + inner, 0)
        return at(zz, yy, c), at(zz, yy, 1 - c), u, along, over, handed, kept, across, served

    loads = []
    for a, src in enumerate((resid, samples)):
        for p in range(2):
            loads.append(
                pltpu.make_async_copy(src.at[:, p], own.at[b, p, :, a], fill.at[0])
            )
    for load in loads:
        load.start()
    load_weights = pltpu.make_async_copy(weights, held, fill.at[1])

    barrier = pltpu.get_barrier_semaphore()

    def greet(**device):
        pl.semaphore_signal(barrier, inc=1, device_id=device, device_id_type=MESH)

    greet(blk=nb)
    greet(wide=y_target)
    greet(wide=c_target)
    greet(wide=in_target)

    @pl.when(inner == 1)
    def _():
        greet(wide=out_target)

    greet(wide=at(outward, y, 1 - c))
    greet(wide=at(z, 1 - y, 1 - c))
    pl.semaphore_wait(barrier, 6 + inner)

    def whole(ref, sent_sem, took_sem):
        return pltpu.make_async_remote_copy(
            src_ref=ref, dst_ref=ref, send_sem=sent_sem, recv_sem=took_sem,
            device_id={"wide": y_target}, device_id_type=MESH,
        )

    def took(ref, sem):
        whole(ref, sends.at[0], sem).wait_recv()

    def sent(ref, k):
        whole(ref, sends.at[k], recv.at[0, 0, 0]).wait_send()

    def push(h, u, src, panel, lane, target):
        sem = beside_cols.at[panel // 2, u] if lane == CORE else recv.at[h, panel // 2, u]
        return pltpu.make_async_remote_copy(
            src_ref=src, dst_ref=cols.at[h, panel, u], send_sem=sends.at[lane],
            recv_sem=sem, device_id={"wide": target}, device_id_type=MESH,
        )

    def arrive(h, u, panel):
        took(cols.at[h, panel, u], recv.at[h, panel // 2, u])

    def arrive_beside(u, panel):
        took(cols.at[:, panel, u], beside_cols.at[panel // 2, u])

    def own_pushes(h, u):
        src = own.at[h, b, u]
        return (
            (None, push(h, u, src, w, OVER, y_target)),
            (None, push(h, u, src, w, ALONG, in_target)),
            (None, push(h, u, src, w, CORE, c_target)),
        ) + (((inner == 1, push(h, u, src, w, ALONG, out_target)),) if u == 0 else ())

    def step_pushes(h, step):
        panel, _, u, along, over = step[:5]
        src = cols.at[h, panel, u]
        target = jnp.where(along == 1, in_target, out_target)
        return (
            (along % 3 > 0, push(h, u, src, panel, ALONG, target)),
            (over == 1, push(h, u, src, panel, OVER, y_target)),
            (None, push(h, u, src, panel, CORE, c_target)),
        )

    def beside_push(h):
        return ((None, pltpu.make_async_remote_copy(
            src_ref=own.at[h, nb], dst_ref=beside.at[h], send_sem=sends.at[BESIDE],
            recv_sem=beside_recv.at[0], device_id={"wide": c_target}, device_id_type=MESH,
        )),)

    def near_push(h, d, u, src, target):
        return ((None, pltpu.make_async_remote_copy(
            src_ref=src, dst_ref=near.at[h, d, u], send_sem=sends.at[NEAR],
            recv_sem=near_recv.at[u if d == 0 else 2], device_id={"wide": target}, device_id_type=MESH,
        )),)

    def near_own(h, u):
        return near_push(h, 0, u, own.at[h, nb, u], y_target)

    def near_relay(h, u):
        return near_push(h, 1, u, near.at[h, 0, u], c_target)

    def near_arrive(u):
        took(near.at[:, 0, u], near_recv.at[u])

    def pair_push(h, d, src, target):
        return ((None, pltpu.make_async_remote_copy(
            src_ref=src, dst_ref=pair.at[h, d], send_sem=sends.at[PAIR],
            recv_sem=pair_recv.at[d], device_id={"wide": target}, device_id_type=MESH,
        )),)

    def pair_own(h):
        return pair_push(h, 0, own.at[h, nb, per - 1], in_target)

    def pair_relay(h):
        return pair_push(h, 1, pair.at[h, 0], c_target)

    def pair_arrive(d):
        took(pair.at[:, d], pair_recv.at[d])

    def share():
        return pltpu.make_async_remote_copy(
            src_ref=shared.at[0], dst_ref=shared.at[1], send_sem=sends.at[SHARE],
            recv_sem=got_recv.at[2], device_id={"wide": at(z, 1 - y, jnp.where(y == 0, c, 1 - c))},
            device_id_type=MESH,
        )

    def hands(handed, d):
        alone = jnp.where(handed == 2, 1, jnp.where(handed >= 3, y, -1))
        return jnp.logical_or(handed == 1, alone == d)

    def lower(handed, d):
        return jnp.where(handed == 4, jnp.where(d == y, 0, 1), 0) == 1

    def cross(h, d, src, target):
        return pltpu.make_async_remote_copy(
            src_ref=src, dst_ref=crossed.at[h, d], send_sem=sends.at[CROSS],
            recv_sem=crossed_recv.at[d], device_id={"wide": target}, device_id_type=MESH,
        )

    def outward_core(d):
        return at(outward, y, jnp.where(d == 0, c, 1 - c))

    def direct(d, p, u, t):
        return pltpu.make_async_remote_copy(
            src_ref=out.at[0, d, p, u, t], dst_ref=got.at[d, p, u, t],
            send_sem=sends.at[DIRECT], recv_sem=got_recv.at[0],
            device_id={"wide": outward_core(d)}, device_id_type=MESH,
        )

    def via(d, p, u):
        return pltpu.make_async_remote_copy(
            src_ref=out.at[1, d, p, u, per - 1], dst_ref=passing.at[d, p, u],
            send_sem=sends.at[VIA], recv_sem=passing_recv.at[p * (1 + u)],
            device_id={"wide": y_target}, device_id_type=MESH,
        )

    def onward(d, p, u):
        return pltpu.make_async_remote_copy(
            src_ref=passing.at[d, p, u], dst_ref=got.at[2 + d, p, u, per - 1],
            send_sem=sends.at[ONWARD], recv_sem=got_recv.at[1],
            device_id={"wide": outward_core(d)}, device_id_type=MESH,
        )

    def start(pushes):
        for when, copy in pushes:
            if when is None:
                copy.start()
            else:
                pl.when(when)(copy.start)

    def swap(h, i, t):
        p = (nb, b)[i] if h is b else (b, nb)[i]
        return pltpu.make_async_remote_copy(
            src_ref=own.at[h, p, t], dst_ref=own.at[h, p, t], send_sem=sends.at[SWAP],
            recv_sem=own_recv.at[2 * i + t], device_id={"blk": nb}, device_id_type=MESH,
        )

    def hand(panel, u):
        return pltpu.make_async_remote_copy(
            src_ref=stage.at[panel, u], dst_ref=landed.at[panel, u],
            send_sem=sends.at[HAND], recv_sem=res_recv.at[panel // 2, u],
            device_id={"blk": nb}, device_id_type=MESH,
        )

    def gram(p, side):
        total = None
        for h in range(2):
            for a in range(2):
                left = own[h, p, :, a].reshape(per * tile, -1)
                right = side(h, 1 - a).reshape(-1, own.shape[5])
                part = lax.dot_general(
                    left, right, (((1,), (1,)), ((), ())), preferred_element_type=jnp.float32
                )
                total = part if total is None else total + part
        return total * scale

    def finish(p, panel, u, part, diagonal=False, rows=None):
        for t in range(per) if rows is None else rows:
            slot = panel * per + u
            weight = held[t, p, slot]
            half = part(t) + RIDGE * weight
            if diagonal and t == u:
                lines = lax.broadcasted_iota(jnp.int32, (tile, tile), 0)
                columns = lax.broadcasted_iota(jnp.int32, (tile, tile), 1)
                on_diag = lines == columns + b * (2 * tile)
                inverse = jnp.where(on_diag, 1.0 / jnp.where(on_diag, weight, 1.0), 0.0)
                stepped = weight - STEP * (half - inverse)
            else:
                stepped = weight - STEP * half
            bound = STEP * LASSO
            updated = stepped - jnp.clip(stepped, -bound, bound)
            if diagonal and t == u:
                updated = jnp.where(on_diag, stepped, updated)
            flag = flags[2 * t + p, slot].astype(jnp.float32)
            held[t, p, slot] = updated * flag

    def cut(total, u=0):
        return lambda t: total[t * tile:(t + 1) * tile, u * tile:(u + 1) * tile]

    def finish_all(p, panel, total, diagonal=False):
        for u in range(per):
            finish(p, panel, u, cut(total, u), diagonal)

    def keep(panel):
        total = gram(0, lambda h, a: cols[h, panel, :, a])
        finish_all(0, panel, total)
        return total

    def emit(across, d, p, u, part):
        t = per - 1
        out[across, d, p, u, t] = part(t).T

        @pl.when(across == 1)
        def _():
            via(d, p, u).start()

        @pl.when(jnp.where(across + d == 0, nb, -1) == p)
        def _():
            for t in range(per - 1):
                out[0, d, p, u, t] = part(t).T

    def pass_on(h, step):
        arrive(h, step[2], step[0])
        start(step_pushes(h, step))

    def piece(ref, h, panel, u, j):
        return ref.at[h, panel, u, :, pl.ds(j * (tile // PARTS), tile // PARTS)]

    def half_push(h, panel, u, j, lane, target):
        sem = halves.at[PARTS + j] if lane == CORE else halves.at[j]
        return pltpu.make_async_remote_copy(
            src_ref=piece(cols, h, panel, u, j), dst_ref=piece(cols, h, panel, u, j),
            send_sem=sends.at[lane], recv_sem=sem, device_id={"wide": target},
            device_id_type=MESH,
        )

    def half_hand(panel, u, j):
        rows = pl.ds(j * (tile // PARTS), tile // PARTS)
        return pltpu.make_async_remote_copy(
            src_ref=stage.at[panel, u, :, rows], dst_ref=landed.at[panel, u, :, rows],
            send_sem=sends.at[HAND], recv_sem=res_recv.at[panel // 2, u],
            device_id={"blk": nb}, device_id_type=MESH,
        )

    def by_halves(step):
        u = step[2]
        for j in range(PARTS):
            rows = pl.ds(j * (tile // PARTS), tile // PARTS)
            for d in range(2):
                panel = step[d]
                took(cols.at[:, panel, u, :, rows], halves.at[PARTS * d + j])
                if d == 0:
                    for h in (b, nb):
                        half_push(h, panel, u, j, CORE, c_target).start()
                total = None
                for h in range(2):
                    for a in range(2):
                        part = lax.dot_general(
                            cols[h, panel, u, a, rows],
                            own[h, 1, :, 1 - a].reshape(per * tile, -1),
                            (((1,), (1,)), ((), ())), preferred_element_type=jnp.float32,
                        )
                        total = part if total is None else total + part
                total = total * scale
                for t in range(per):
                    stage[panel, u, t, rows] = total[:, t * tile:(t + 1) * tile]
                half_hand(panel, u, j).start()

    def forward(n):
        step = decode(n)

        @pl.when(step[3] < 3)
        def _():
            for h in (b, nb):
                pass_on(h, step)

        @pl.when(step[4] == 2)
        def _():
            for j in range(PARTS):
                for h in (b, nb):
                    half_push(h, step[0], step[2], j, OVER, y_target).start()

    pltpu.make_async_copy(own.at[b], own.at[b], fill.at[0]).wait()
    for i in range(2):
        for t in range(per):
            swap(b, i, t).start()
    for t in range(per):
        start(own_pushes(b, t))
    load_weights.start()
    start(beside_push(b))
    for t in range(per):
        swap(nb, 0, t).wait_recv()
        start(own_pushes(nb, t))

    def early(n, carry):
        forward(n)
        return carry

    def reached(n):
        mid = jnp.where(n < 12, 3 * (jnp.maximum(n, 0) // 3) + 3, n + 1)
        return jnp.maximum(ahead, jnp.where(inner == 1, mid, n + 1))

    def row_hand(panel, u, t, lane=HAND):
        total = None
        for h in range(2):
            for a in range(2):
                part = lax.dot_general(
                    own[h, 1, t, a], cols[h, panel, u, 1 - a], (((1,), (1,)), ((), ())),
                    preferred_element_type=jnp.float32,
                )
                total = part if total is None else total + part
        stage[panel, u, t] = total * scale
        pltpu.make_async_remote_copy(
            src_ref=stage.at[panel, u, t], dst_ref=landed.at[panel, u, t],
            send_sem=sends.at[lane], recv_sem=res_recv.at[panel // 2, u],
            device_id={"blk": nb}, device_id_type=MESH,
        ).start()

    lax.fori_loop(0, 2, early, 0)
    took(own.at[nb, nb, 0], own_recv.at[2])

    @pl.when(inner == 0)
    def _():
        def first_row(n, carry):
            first, second, u = decode(n)[:3]
            arrive_beside(u, second)
            row_hand(jnp.where(jnp.where(n == 0, y, 1) == 0, first, second), u, 0)
            return carry

        lax.fori_loop(0, 2, first_row, 0)

    lax.fori_loop(2, ahead, early, 0)
    for t in range(1, per):
        took(own.at[nb, nb, t], own_recv.at[2 + t])

    @pl.when(inner == 0)
    def _():
        for h in (b, nb):
            cross(h, 0, own.at[h, nb, per - 1], in_target).start()
    start(beside_push(nb))
    load_weights.wait()

    def receive(n):
        step = decode(n)
        u, handed, across, served = step[2], step[5], step[7], step[8]

        chip = step[0] // 2

        @pl.when(handed == 1)
        def _():
            took(landed.at[pl.ds(2 * chip, 2), u], res_recv.at[chip, u])

        @pl.when(jnp.where(handed == 4, 0, handed) > 1)
        def _():
            took(landed.at[0, u], res_recv.at[chip, u])

        @pl.when(handed == 4)
        def _():
            took(held.at[0, 0, :3], res_recv.at[chip, u])

        for d in range(2):
            panel = step[d]

            @pl.when(lower(handed, d))
            def _():
                finish(1, panel, u, lambda t: landed[panel, u, t], rows=(per - 1,))

            @pl.when(step[3] == 3)
            def _():
                finish(1, panel, u, lambda t: landed[panel, u, t].T)

            @pl.when(hands(jnp.where(step[3] == 3, 0, handed), d))
            def _():
                finish(1, panel, u, lambda t: landed[panel, u, t])

                @pl.when(served == 2)
                def _():
                    emit(across, d, 1, u, lambda t: landed[panel, u, t])

                @pl.when(jnp.where(served == 1, nb + jnp.where(d == y, 1, 0), 0) == 2)
                def _():
                    for t in range(per):
                        shared[0, 2 * t + u] = landed[panel, u, t].T

    def settle(n, carry):
        receive(n)
        return carry

    def nearby():
        for p in range(2):
            parity = b if p == 0 else nb
            finish_all(p, w, gram(p, lambda h, a: own[h, parity, :, a]), True)
        for u in range(per):
            arrive_beside(u, c_target)
        took(beside, beside_recv.at[0])
        keep(c_target)
        finish_all(1, c_target, gram(1, lambda h, a: beside[h, :, a]))

    def compute(n, carry):
        lax.fori_loop(reached(n - 1), reached(n), early, 0)

        step = decode(n)
        first, second, u, along, _, handed, kept, across, served = step

        begun = jnp.logical_and(n < 2, inner == 0)

        @pl.when(along == 3)
        def _():
            by_halves(step)

        def both(i, carry):
            panel = jnp.where(i == 0, first, second)

            @pl.when(jnp.where(along == 3, 0, jnp.where(begun, 0, i)) == 1)
            def _():
                arrive_beside(u, panel)

            @pl.when(hands(jnp.where(begun, handed, 0), i))
            def _():
                for t in range(1, per):
                    row_hand(panel, u, t)

            @pl.when(hands(jnp.where(along == 3, 0, jnp.where(begun, 0, handed)), i))
            def _():
                total = cut(gram(1, lambda h, a: cols[h, panel, u, a]))
                for t in range(per):
                    stage[panel, u, t] = total(t)
                hand(panel, u).start()

            @pl.when(lower(handed, i))
            def _():
                row_hand(panel, u, per - 1, SHARE)

            @pl.when(kept == 1)
            def _():
                total = keep(panel)

                @pl.when(served == 2)
                def _():
                    for v in range(per):
                        emit(across, i, 0, v, cut(total, v))

                @pl.when(jnp.where(served == 1, nb + jnp.where(i == y, 0, 1), 1) == 0)
                def _():
                    for v in range(per):
                        for t in range(per):
                            shared[0, 2 * t + v] = cut(total, v)(t).T

            @pl.when(kept == 2)
            def _():
                finish(0, panel, u, cut(gram(0, lambda h, a: cols[h, panel, u, a])))

            return carry

        lax.fori_loop(0, 2, both, 0)

        @pl.when(n == ahead - 1)
        def _():
            nearby()

        @pl.when(n == BATCH)
        def _():
            lax.fori_loop(0, BATCH - LAG, settle, 0)

        @pl.when(n >= BATCH)
        def _():
            receive(n - LAG)

        @pl.when(jnp.where(inner == 0, n, -1) == BATCH + 1)
        def _():
            share().start()

        @pl.when(inner == 1)
        def _():
            @pl.when(n == STEPS - 9)
            def _():
                for h in (b, nb):
                    start(near_own(h, 0))

            @pl.when(n == STEPS - 7)
            def _():
                start(near_own(b, 1))

            @pl.when(n == BATCH + 1)
            def _():
                for d in range(2):
                    direct(d, 0, 0, per - 1).start()
                    direct(d, 1, 0, per - 1).start()
                    direct(d, 0, 1, per - 1).start()
                direct(0, nb, 0, 0).start()

                @pl.when(nb == 0)
                def _():
                    direct(0, 0, 1, 0).start()

            @pl.when(n == STEPS - 4)
            def _():
                start(near_own(nb, 1))
                for h in (b, nb):
                    start(pair_own(h))

            @pl.when(n == STEPS - 3)
            def _():
                took(crossed.at[:, 0], crossed_recv.at[0])
                for h in (b, nb):
                    cross(h, 1, crossed.at[h, 0], c_target).start()

            @pl.when(n == STEPS - 2)
            def _():
                took(crossed.at[:, 1], crossed_recv.at[1])

            @pl.when(jnp.logical_or(n == STEPS - 3, n == STEPS - 2))
            def _():
                d = n - (STEPS - 3)
                total = cut(gram(1, lambda h, a: crossed[h, d, a]))
                finish(1, at(outward, y, jnp.where(d == 0, c, 1 - c)), per - 1, total)
                emit(0, d, 1, per - 1, total)
                direct(d, 1, per - 1, per - 1).start()

                @pl.when(jnp.where(d == 0, nb, 0) == 1)
                def _():
                    direct(0, 1, per - 1, 0).start()

            @pl.when(n == STEPS - 2)
            def _():
                relay(0)

            @pl.when(n == STEPS - 1)
            def _():
                relay(1)

        return carry

    def relay(k):
        p = min(k, 1)
        tiles = range(per) if k == 0 else (k - 1,)
        took(passing.at[:, p] if k == 0 else passing.at[:, p, k - 1], passing_recv.at[k])
        for u in tiles:
            for d in range(2):
                onward(d, p, u).start()

    lax.fori_loop(0, count, compute, 0)

    @pl.when(inner == 1)
    def _():
        near_arrive(0)
        for h in (b, nb):
            start(near_relay(h, 0))
        relay(2)
        receive(count - LAG)
        lax.fori_loop(count - LAG + 1, count - 2, settle, 0)
        near_arrive(1)
        for h in (b, nb):
            start(near_relay(h, 1))
        pair_arrive(0)
        for h in (b, nb):
            start(pair_relay(h))

        def adjacent(d, carry):
            cc = jnp.where(d == 0, c, 1 - c)

            @pl.when(d == 1)
            def _():
                took(near.at[:, 1], near_recv.at[2])
                pair_arrive(1)

            finish_all(1, at(z, 1 - y, cc), gram(1, lambda h, a: near[h, d, :, a]))
            finish(1, at(inward, y, cc), per - 1, cut(gram(1, lambda h, a: pair[h, d, a])))
            return carry

        lax.fori_loop(0, 2, adjacent, 0)

        sent(held.at[:, 0, :5], DIRECT)
        sent(passing, VIA)
        sent(passing, ONWARD)
        sent(near, NEAR)
        sent(pair, PAIR)
        sent(crossed.at[:, 0], CROSS)
        sent(cols.at[0, :11], ALONG)
        sent(cols.at[0, :4], OVER)
        sent(cols.at[:, :8], CORE)

    @pl.when(inner == 0)
    def _():
        def accept(k, t, p):
            d = k % 2
            panel = at(inward, jnp.where(k < 2, y, 1 - y), jnp.where(d == 0, c, 1 - c))
            finish(jnp.where(p == 0, b, nb), panel, t, lambda u: got[k, p, u, t])

        def closer(k, carry):
            @pl.when(k == 0)
            def _():
                for t in range(per - 1):
                    accept(k, t, nb)

            for p in range(2):
                accept(k, per - 1, p)
            return carry

        def farther(k, carry):
            accept(k % 2 + 2, per - 1, k // 2)
            return carry

        lax.fori_loop(count - LAG, count - 2, settle, 0)
        took(held.at[:, 0, :5], got_recv.at[0])
        lax.fori_loop(0, 2, closer, 0)
        took(got.at[2:, :, :, per - 1], got_recv.at[1])
        lax.fori_loop(0, 4, farther, 0)
        sent(cols.at[0, :4], ALONG)
        sent(cols.at[0, :7], OVER)
        sent(cols.at[:, :7], CORE)
        took(shared.at[1], got_recv.at[2])
        other = at(z, 1 - y, jnp.where(y == 1, c, 1 - c))
        for u in range(per):
            finish(1, other, u, lambda t: shared[1, 2 * u + t])
        sent(held.at[0, 0, :4], SHARE)
        sent(crossed.at[:, 0], CROSS)

    sent(own.at[b], SWAP)
    sent(beside, BESIDE)
    lax.fori_loop(count - 2, count, settle, 0)

    @pl.when(inner == 0)
    def _():
        sent(held.at[:, 0, :21], HAND)

    @pl.when(inner == 1)
    def _():
        sent(held.at[:, 0, :20], HAND)


def ring(resid, samples, precision, active):
    panels = lax.axis_size("wide")
    row_tiles, _, per_class, tile, _ = precision.shape
    per = row_tiles // 2
    half = resid.shape[1]
    depth = panels // 4
    scale = 0.5 / (2 * half)
    any_spec = pl.BlockSpec(memory_space=pl.ANY)
    bf16, f32 = resid.dtype, jnp.float32
    dma = pltpu.SemaphoreType.DMA
    updated = pl.pallas_call(
        functools.partial(kernel, depth, scale),
        out_shape=pltpu.VMEM((per, 2, per_class, tile, tile), f32),
        in_specs=[any_spec, any_spec, any_spec, pl.BlockSpec(memory_space=pltpu.SMEM)],
        out_specs=pl.BlockSpec(memory_space=pltpu.VMEM),
        scratch_shapes=[
            pltpu.VMEM((2, 2, per, 2, tile, half), bf16),
            pltpu.VMEM((2, panels, per, 2, tile, half), bf16),
            pltpu.VMEM((2, per, 2, tile, half), bf16),
            pltpu.VMEM((2, 2, per, 2, tile, half), bf16),
            pltpu.VMEM((2, 2, 2, tile, half), bf16),
            pltpu.VMEM((panels, per, per, tile, tile), f32),
            pltpu.VMEM((panels, per, per, tile, tile), f32),
            pltpu.VMEM((2, 2, 2, per, per, tile, tile), f32),
            pltpu.VMEM((4, 2, per, per, tile, tile), f32),
            pltpu.VMEM((2, 2, per, tile, tile), f32),
            pltpu.VMEM((2, 2 * per, tile, tile), f32),
            pltpu.VMEM((2, 2, 2, tile, half), bf16),
            dma((2, panels // 2, per)),
            dma((panels // 2, per)),
            dma((4,)),
            dma((panels // 2, per)),
            dma((2 * PARTS,)),
            dma((1,)),
            dma((3,)),
            dma((2,)),
            dma((3,)),
            dma((3,)),
            dma((13,)),
            dma((2,)),
            dma((2,)),
        ],
        compiler_params=pltpu.CompilerParams(
            collective_id=0, has_side_effects=True, vmem_limit_bytes=52 * 1024 * 1024
        ),
    )(
        resid.reshape(per, 2, tile, half),
        samples.reshape(per, 2, tile, half),
        precision.reshape(per, 2, per_class, tile, tile),
        active[:, 0],
    )
    return updated.reshape(precision.shape)


def body(resid, samples, precision, active):
    panels = lax.axis_size("wide")
    row_tiles, _, per_class, tile, _ = precision.shape
    words = 8 * per_class * row_tiles * tile * tile + 4 * panels * row_tiles * tile * resid.shape[1]
    if lax.axis_size("blk") == 2 and panels // 4 == 4 and row_tiles == 4 and words < 52 * 1024 * 1024:
        return ring(resid, samples, precision, active)
    return local(resid, samples, precision, active)


def solution(mesh):
    in_specs = (
        P("wide", "blk"),
        P("wide", "blk"),
        P("wide", "blk", None, None, None),
        P("wide", "blk", None),
    )
    out_specs = P("wide", "blk", None, None, None)
    return jax.shard_map(body, mesh=mesh, in_specs=in_specs, out_specs=out_specs, check_vma=False)
```
